256 devices in a mesh: seq: 32 (over z, y), dp: 8 (over x, core).
Axes of the slice: x: 4, y: 4, z: 8, core: 2. Of those that a mesh axis runs over, the one named last changes fastest.
Arguments:
- byte_states: bfloat16 [8, 8192, 4096], P('dp', 'seq'), may hold values from -16 to 16
- byte_patch: int32 [8, 8192], P('dp', 'seq'), may hold values from 0 to 2111, as said below
- patch_owner: int32 [8, 2112], P('dp'), may hold values from 0 to 31, as said below
- qkv_weight: bfloat16 [4096, 3072], P(None, 'dp'), may hold values from -0.09375 to 0.09375
- attention_output_gradient: bfloat16 [8, 2112, 2048], P('dp', 'seq'), may hold values from -6 to 6
Outputs:
- attention: bfloat16 [8, 2112, 2048], P('dp', 'seq')
- state_grad: bfloat16 [8, 8192, 4096], P('dp', 'seq')
- weight_grad: float32 [4096, 3072], P('seq', 'dp')
The draws below stay inside these ranges and needn't reach their ends.
Inputs may be any that keep to these rules, and one draw needn't show every extreme that they name: `byte_patch`: patch numbers never fall along a sequence, every patch lies within the bytes of one index of seq, and every patch number is used. One index of seq in each sequence, drawn, holds 128 patches of two bytes; every other index holds 64 patches in consecutive pairs that together hold 8 bytes, each patch 1 to 7 bytes. `patch_owner`: patches 0 to 31, 32 to 63 and so on form groups in which every owner appears exactly once.
All inputs are finite; a program needn't handle non-finite values.
Results may differ from the reference program's by a relative error of at most 0.028.
Values may be sent and summed in bfloat16 or wider, within the bound.
A program may use at most 128 MiB of HBM per device.

```python
import jax
import jax.numpy as jnp
from jax import lax

DG = 4096
QUERY_HEADS = 16
KEY_VALUE_HEADS = 4
HEAD_SIZE = 128
PIECE_CHARACTERS = 256
STRAND_TALLY = 8
LEN = 8192
SEQUENCE_PATCHES = 2112
OWNER_PATCHES = 66
QKV = 3072
COLS = 384
N_SEQ = 32
N_DP = 8


def patch_layout(key):
    spike_piece_position = jax.random.randint(jax.random.fold_in(key, 11), (STRAND_TALLY,), 0, N_SEQ)
    firsts = jax.random.randint(jax.random.fold_in(key, 12), (STRAND_TALLY, N_SEQ, PIECE_CHARACTERS // 8), 1, 8)
    beginning_displacements = jnp.arange(PIECE_CHARACTERS, dtype=jnp.int32)
    pair_index = beginning_displacements // 8
    within = beginning_displacements % 8
    gaussian_draw = 2 * pair_index[None, None, :] + (within[None, None, :] >= firsts[:, :, pair_index]).astype(jnp.int32)
    spike_member_entries = beginning_displacements // 2
    piece_tally = jnp.arange(N_SEQ, dtype=jnp.int32)
    within_spike = piece_tally[None, :] == spike_piece_position[:, None]
    foremost_entry = piece_tally[None, :] * (PIECE_CHARACTERS // 4) + (piece_tally[None, :] > spike_piece_position[:, None]).astype(jnp.int32) * (PIECE_CHARACTERS // 4)
    hosted_segment = jnp.where(within_spike[:, :, None], spike_member_entries[None, None, :], gaussian_draw)
    byte_patch = (foremost_entry[:, :, None] + hosted_segment).reshape(STRAND_TALLY, LEN).astype(jnp.int32)
    ranked = jax.random.randint(jax.random.fold_in(key, 13), (STRAND_TALLY, OWNER_PATCHES, N_SEQ), 0, 1 << 20) * N_SEQ + piece_tally[None, None, :]
    owner_order = jnp.argsort(ranked, axis=-1, stable=True).astype(jnp.int32)
    return (byte_patch, owner_order.reshape(STRAND_TALLY, SEQUENCE_PATCHES))


def draw_byte_patch(key, part):
    return patch_layout(key)[0]


def draw_patch_owner(key, part):
    return patch_layout(key)[1]


def draw_byte_states(key, part):
    key_noise = jax.random.fold_in(key, 21)
    value_rows = jnp.clip(jax.random.normal(key_noise, (STRAND_TALLY, LEN, DG), jnp.float32), -6.0, 6.0)
    return jnp.clip(value_rows, -16.0, 16.0).astype(jnp.bfloat16)


def levels(key, shape, cuts, low, high):
    gain, own = 1.0, jax.random.fold_in(key, 6)
    for position, parts in cuts:
        draws = jnp.exp(jax.random.uniform(jax.random.fold_in(own, position), (parts,), jnp.float32, low / len(cuts), high / len(cuts)))
        gain = gain * jnp.repeat(draws, shape[position] // parts).reshape([-1 if axis == position else 1 for axis in range(len(shape))])
    return gain


def scatter_about(own_key, extent, width, reach, cuts=(), kind=jnp.bfloat16):
    array = jax.random.normal(own_key, extent, jnp.float32) * width
    if len(cuts) > 0:
        array = levels(own_key, extent, cuts, -0.22, 0.18) * array
    return jnp.clip(array, min=-reach, max=reach).astype(kind)


def setup_inputs(seed: int = 0) -> dict:
    seeds = jax.random.split(jax.random.key(seed), 6)
    return {
        "byte_states": draw_byte_states(jax.random.fold_in(seeds[5], 71), 0),
        "byte_patch": draw_byte_patch(jax.random.fold_in(seeds[5], 71), 0),
        "patch_owner": draw_patch_owner(jax.random.fold_in(seeds[5], 71), 0),
        "qkv_weight": scatter_about(seeds[3], (DG, QKV), DG ** -0.5, 0.09375, ((1, 8),)),
        "attention_output_gradient": scatter_about(seeds[4], (STRAND_TALLY, SEQUENCE_PATCHES, QUERY_HEADS * HEAD_SIZE), 1.0, 6.0, ((0, 8), (1, 32))),
    }


def contract_rows(left, right):
    return lax.dot_general(left, right, (((0,), (0,)), ((), ())), preferred_element_type=jnp.float32)


def one_sequence(states, patch_ids, owners, qkv_weight, output_cotangent):
    unit_terms = jnp.ones((LEN,), jnp.float32)
    counts = jax.ops.segment_sum(unit_terms, patch_ids, num_segments=SEQUENCE_PATCHES)
    summed = jax.ops.segment_sum(states.astype(jnp.float32), patch_ids, num_segments=SEQUENCE_PATCHES)
    pooled = (summed / jnp.maximum(counts, 1.0)[:, None]).astype(jnp.bfloat16)
    patch_order = jnp.arange(SEQUENCE_PATCHES, dtype=jnp.int32)
    placed = (owners * OWNER_PATCHES + patch_order // N_SEQ).astype(jnp.int32)
    own_rows = jnp.zeros_like(pooled).at[placed].set(pooled)
    own_index = jnp.zeros((SEQUENCE_PATCHES,), jnp.int32).at[placed].set(patch_order)
    projected_states = jnp.dot(own_rows, qkv_weight, preferred_element_type=jnp.float32).astype(jnp.bfloat16)
    query_group_size = QUERY_HEADS // KEY_VALUE_HEADS
    query_row_width = QUERY_HEADS * HEAD_SIZE
    key_row_width = KEY_VALUE_HEADS * HEAD_SIZE
    query_rows = projected_states[:, :query_row_width].reshape(SEQUENCE_PATCHES, KEY_VALUE_HEADS, query_group_size, HEAD_SIZE).astype(jnp.float32)
    key_head_count = projected_states[:, query_row_width:query_row_width + key_row_width].reshape(SEQUENCE_PATCHES, KEY_VALUE_HEADS, HEAD_SIZE).astype(jnp.float32)
    value_rows = projected_states[:, query_row_width + key_row_width:].reshape(SEQUENCE_PATCHES, KEY_VALUE_HEADS, HEAD_SIZE).astype(jnp.float32)
    factor = HEAD_SIZE ** -0.5
    scores = jnp.einsum('qhgd,khd->hgqk', query_rows, key_head_count) * factor
    allowed = own_index[None, :] <= own_index[:, None]
    scores = jnp.where(allowed[None, None], scores, -jnp.inf)
    row_peak = jnp.max(scores, axis=-1, keepdims=True)
    shifted = jnp.exp(scores - row_peak)
    attend = shifted / jnp.sum(shifted, axis=-1, keepdims=True)
    attended_lower = attend.astype(jnp.bfloat16).astype(jnp.float32)
    attended = jnp.einsum('hgqk,khd->qhgd', attended_lower, value_rows)
    attention = attended.reshape(SEQUENCE_PATCHES, query_row_width).astype(jnp.bfloat16)
    gradient_row_list = output_cotangent.astype(jnp.float32).reshape(SEQUENCE_PATCHES, KEY_VALUE_HEADS, query_group_size, HEAD_SIZE)
    grad_attend = jnp.einsum('qhgd,khd->hgqk', gradient_row_list, value_rows)
    row_delta = jnp.einsum('qhgd,qhgd->hgq', gradient_row_list, attended)
    score_gradient = (attend * (grad_attend - row_delta[..., None])).astype(jnp.bfloat16).astype(jnp.float32)
    grad_queries = jnp.einsum('hgqk,khd->qhgd', score_gradient, key_head_count) * factor
    score_block_list = score_gradient.reshape(KEY_VALUE_HEADS, query_group_size, N_SEQ, OWNER_PATCHES, SEQUENCE_PATCHES)
    attended_block_list = attended_lower.reshape(KEY_VALUE_HEADS, query_group_size, N_SEQ, OWNER_PATCHES, SEQUENCE_PATCHES)
    query_block_list = query_rows.reshape(N_SEQ, OWNER_PATCHES, KEY_VALUE_HEADS, query_group_size, HEAD_SIZE)
    gradient_block_list = gradient_row_list.reshape(N_SEQ, OWNER_PATCHES, KEY_VALUE_HEADS, query_group_size, HEAD_SIZE)
    key_part = (jnp.einsum('hgiqk,iqhgd->ikhd', score_block_list, query_block_list) * factor).astype(jnp.bfloat16).astype(jnp.float32)
    grad_keys = jnp.sum(key_part, axis=0)
    value_part = jnp.einsum('hgiqk,iqhgd->ikhd', attended_block_list, gradient_block_list).astype(jnp.bfloat16).astype(jnp.float32)
    grad_values = jnp.sum(value_part, axis=0)
    grad_proj = jnp.concatenate([grad_queries.reshape(SEQUENCE_PATCHES, query_row_width), grad_keys.reshape(SEQUENCE_PATCHES, key_row_width), grad_values.reshape(SEQUENCE_PATCHES, key_row_width)], axis=1).astype(jnp.bfloat16)
    grad_split = grad_proj.reshape(SEQUENCE_PATCHES, N_DP, COLS).astype(jnp.float32)
    weight_split = qkv_weight.reshape(DG, N_DP, COLS).astype(jnp.float32)
    pooled_part = jnp.einsum('pic,gic->ipg', grad_split, weight_split).astype(jnp.bfloat16).astype(jnp.float32)
    grad_pooled = jnp.sum(pooled_part, axis=0).astype(jnp.bfloat16)
    per_patch = grad_pooled[placed].astype(jnp.float32) / jnp.maximum(counts, 1.0)[:, None]
    state_grad = per_patch[patch_ids].astype(jnp.bfloat16)
    return attention, state_grad, own_rows, grad_proj


def reference(byte_states, byte_patch, patch_owner, qkv_weight, attention_output_gradient):
    outputs = []
    grads = []
    row_list = []
    proj_list = []
    for index_seq in range(STRAND_TALLY):
        attention, state_grad, own_rows, grad_proj = one_sequence(byte_states[index_seq], byte_patch[index_seq], patch_owner[index_seq], qkv_weight, attention_output_gradient[index_seq])
        outputs.append(attention)
        grads.append(state_grad)
        row_list.append(own_rows)
        proj_list.append(grad_proj)
    row_blocks = jnp.stack(row_list).reshape(STRAND_TALLY, N_SEQ, OWNER_PATCHES, DG).transpose(1, 0, 2, 3).reshape(N_SEQ, STRAND_TALLY * OWNER_PATCHES, DG)
    proj_blocks = jnp.stack(proj_list).reshape(STRAND_TALLY, N_SEQ, OWNER_PATCHES, QKV).transpose(1, 0, 2, 3).reshape(N_SEQ, STRAND_TALLY * OWNER_PATCHES, QKV)

    def add_block(total, pair):
        term = contract_rows(pair[0], pair[1]).astype(jnp.bfloat16).astype(jnp.float32)
        return total + term, None

    weight_grad, unused = lax.scan(add_block, jnp.zeros((DG, QKV), jnp.float32), (row_blocks, proj_blocks))
    return jnp.stack(outputs), jnp.stack(grads), weight_grad
```

```python
import functools

import jax
import jax.numpy as jnp
from jax import lax
from jax.experimental import pallas as pl
from jax.experimental.pallas import tpu as pltpu
from jax.sharding import Mesh
from jax.sharding import PartitionSpec as P

QUERY_HEADS = 16
KEY_VALUE_HEADS = 4
HEAD = 128
FACTOR = HEAD ** (-0.5)
NZ, NY, NX, NC = 8, 4, 4, 2
NS, NDP = NZ * NY, NX * NC
SEQ = ("z", "y")
DP = ("x", "c")
MAIN = 64
BYTES = 256
DG = 4096
PATCHES = 2112
COLS = 384
BF = jnp.bfloat16
F32 = jnp.float32
VMEM_LIMIT = 56 << 20


def dot(a, b):
    return jnp.dot(a, b, preferred_element_type=F32)


def dot_t(a, b):
    return lax.dot_general(a, b, (((0,), (0,)), ((), ())), preferred_element_type=F32)


def pool_kernel(
    ids_ref, owner_ref, states_ref, grad_ref,
    main_ref, over_ref, slot_ref, flag_ref, band_ref,
    onehot_ref,
):
    s = lax.axis_index("z") * NY + lax.axis_index("y")

    @pl.when(pl.program_id(0) == 0)
    def _():
        ids = ids_ref[...]
        first = jnp.min(ids, axis=1, keepdims=True)
        last = jnp.max(ids, axis=1, keepdims=True)
        group = (ids - first) >> 5
        patch = lax.broadcasted_iota(jnp.int32, (PATCHES, BYTES), 0)
        hit = jnp.where(patch == ids, 1.0, 0.0).astype(BF)
        owner = jnp.broadcast_to(owner_ref[...].astype(F32), (16, PATCHES)).astype(BF)
        byte_owner = dot(owner, hit)[0:1].astype(jnp.int32)
        over = MAIN + (byte_owner & 3) * 16 + (byte_owner >> 2) * 2 + (group - 2)
        slot = jnp.where(group < 2, group * 32 + byte_owner, over)
        slot_ref[...] = slot
        rows = lax.broadcasted_iota(jnp.int32, (2 * MAIN, BYTES), 0)
        onehot_ref[...] = jnp.where(rows == slot, 1.0, 0.0)
        spike = jnp.where(last - first >= MAIN, s.astype(F32), 0.0)
        flag_ref[...] = jnp.broadcast_to(spike, (8, 128))

    onehot = onehot_ref[...]
    counts = jnp.maximum(jnp.sum(onehot, axis=1, keepdims=True), 1.0)
    pooled = (dot(onehot.astype(BF), states_ref[0]) / counts).astype(BF)
    main_ref[...] = pooled[:MAIN]
    over_ref[...] = pooled[MAIN:].reshape(NY, 16, pooled.shape[1])
    grad = grad_ref[0]
    for z in range(NZ - 1):
        band_ref[z] = grad[8 * z : 8 * z + 16]
    band_ref[NZ - 1] = jnp.zeros_like(band_ref[NZ - 1])
    band_ref[NZ - 1, 0:10, :] = grad[56:66]


def pool(byte_patch, patch_owner, byte_states, grad):
    steps = 4
    width = DG // steps
    return pl.pallas_call(
        pool_kernel,
        grid=(steps,),
        in_specs=[
            pl.BlockSpec((1, BYTES), lambda i: (0, 0)),
            pl.BlockSpec((1, PATCHES), lambda i: (0, 0)),
            pl.BlockSpec((1, BYTES, width), lambda i: (0, 0, i)),
            pl.BlockSpec((1, 66, 512), lambda i: (0, 0, i)),
        ],
        out_specs=[
            pl.BlockSpec((MAIN, width), lambda i: (0, i)),
            pl.BlockSpec((NY, 16, width), lambda i: (0, 0, i)),
            pl.BlockSpec((1, BYTES), lambda i: (0, 0)),
            pl.BlockSpec((8, 128), lambda i: (0, 0)),
            pl.BlockSpec((NZ, 16, 512), lambda i: (0, 0, i)),
        ],
        out_shape=[
            jax.ShapeDtypeStruct((MAIN, DG), BF),
            jax.ShapeDtypeStruct((NY, 16, DG), BF),
            jax.ShapeDtypeStruct((1, BYTES), jnp.int32),
            jax.ShapeDtypeStruct((8, 128), F32),
            jax.ShapeDtypeStruct((NZ, 16, 2048), BF),
        ],
        scratch_shapes=[pltpu.VMEM((2 * MAIN, BYTES), F32)],
        name="pool",
    )(byte_patch, patch_owner, byte_states, grad)


MESH = pl.DeviceIdType.MESH
ANY = pl.BlockSpec(memory_space=pl.ANY)
VM = pl.BlockSpec(memory_space=pltpu.VMEM)


def here():
    return [lax.axis_index(name) for name in ("z", "y", "x", "c")]


def send(src, dst, pair, **device):
    return pltpu.make_async_remote_copy(
        src_ref=src, dst_ref=dst, send_sem=pair[0], recv_sem=pair[1],
        device_id=device, device_id_type=MESH,
    )


def greet(devices):
    barrier = pltpu.get_barrier_semaphore()
    for device in devices:
        pl.semaphore_signal(barrier, inc=1, device_id=device, device_id_type=MESH)
    pl.semaphore_wait(barrier, len(devices))


def gather_kernel(
    main, over, flag, band,
    all_main, all_over, spot, gy, gz,
    ybuf, zsrc, zbuf, mine, fy, fsum, fz,
    local, main_s, main_r, ys, yr, zs, zr, os_, or_,
):
    z, y, x, c = here()
    n = x * 2 + c
    ys_at = [lax.rem(y + j, NY) for j in range(NY)]
    zs_at = [lax.rem(z + j, NZ) for j in range(NZ)]
    dp_at = [lax.rem(n + j, NDP) for j in range(NDP)]
    right, left, other = lax.rem(x + 1, NX), lax.rem(x + 3, NX), 1 - c
    greet(
        [{"y": ys_at[j]} for j in range(1, NY)]
        + [{"z": zs_at[j]} for j in range(1, NZ)]
        + [{"x": p // 2, "c": lax.rem(p, 2)} for p in dp_at[1:]]
    )

    def half(block, i):
        return block.at[pl.ds(32 * i, 32), :]

    def pair(i):
        return main_s.at[i], main_r.at[i]

    mine_out = all_main.at[n]
    first = [
        send(main, mine_out, pair(1), x=right),
        send(main, mine_out, pair(2), x=left),
        send(main, mine_out, pair(0), c=other),
    ]
    for copy in first:
        copy.start()
    keep = [pltpu.make_async_copy(main, mine_out, local.at[0])]

    stage_y = []
    for j in range(1, NY):
        stage_y.append(send(over.at[ys_at[j]], ybuf.at[y], (ys.at[0, j], yr.at[0, j]), y=ys_at[j]))
        stage_y.append(send(flag, fy.at[y], (ys.at[1, j], yr.at[1, j]), y=ys_at[j]))
    here_y = [
        pltpu.make_async_copy(over.at[y], ybuf.at[y], local.at[1]),
        pltpu.make_async_copy(flag, fy.at[y], local.at[2]),
    ]
    for copy in stage_y + here_y + keep:
        copy.start()

    def columns(h):
        return pl.ds(pl.multiple_of(h * 512, 512), 512)

    grads_y = [
        send(band.at[:, :, columns(ys_at[j])], gy.at[y], (ys.at[2, j], yr.at[2, j]), y=ys_at[j])
        for j in range(1, NY)
    ]
    keep_y = pltpu.make_async_copy(band.at[:, :, columns(y)], gy.at[y], local.at[3])
    for copy in grads_y + [keep_y]:
        copy.start()

    for copy in stage_y:
        copy.wait_recv()
    for copy in here_y:
        copy.wait()
    rows = (
        ybuf[0].astype(F32) + ybuf[1].astype(F32) + ybuf[2].astype(F32) + ybuf[3].astype(F32)
    ).astype(BF)
    for k in range(NZ):
        zsrc[k] = rows[2 * k : 2 * k + 2]
    fsum[...] = fy[0] + fy[1] + fy[2] + fy[3]
    stage_z = []
    for j in range(1, NZ):
        stage_z.append(send(zsrc.at[zs_at[j]], zbuf.at[z], (zs.at[0, j], zr.at[0, j]), z=zs_at[j]))
        stage_z.append(send(fsum, fz.at[z], (zs.at[1, j], zr.at[1, j]), z=zs_at[j]))
    here_z = [
        pltpu.make_async_copy(zsrc.at[z], zbuf.at[z], local.at[4]),
        pltpu.make_async_copy(fsum, fz.at[z], local.at[5]),
    ]
    for copy in stage_z + here_z:
        copy.start()
    for copy in stage_z:
        copy.wait_recv()
    for copy in here_z:
        copy.wait()
    total = zbuf[0].astype(F32)
    found = fz[0]
    for k in range(1, NZ):
        total = total + zbuf[k].astype(F32)
        found = found + fz[k]
    mine[...] = total.astype(BF)
    spot[...] = found
    overs = [
        send(mine, all_over.at[n], (os_.at[j], or_.at[j]), x=dp_at[j] // 2, c=lax.rem(dp_at[j], 2))
        for j in range(1, NDP)
    ]
    keep_o = pltpu.make_async_copy(mine, all_over.at[n], local.at[6])
    for copy in overs + [keep_o]:
        copy.start()

    for copy in grads_y:
        copy.wait_recv()
    keep_y.wait()
    grads_z = [
        send(gy.at[:, zs_at[j]], gz.at[z], (zs.at[2, j], zr.at[2, j]), z=zs_at[j])
        for j in range(1, NZ)
    ]
    keep_z = pltpu.make_async_copy(gy.at[:, z], gz.at[z], local.at[7])
    for copy in grads_z + [keep_z]:
        copy.start()

    from_left = all_main.at[left * 2 + c]
    from_right = all_main.at[right * 2 + c]
    far = all_main.at[lax.rem(x + 2, NX) * 2 + c]
    first[0].wait_recv()
    on_right = send(half(from_left, 0), half(from_left, 0), pair(3), x=right)
    side_left = send(from_left, from_left, pair(5), c=other)
    on_right.start()
    first[1].wait_recv()
    on_left = send(half(from_right, 1), half(from_right, 1), pair(4), x=left)
    side_right = send(from_right, from_right, pair(6), c=other)
    on_left.start()
    side_left.start()
    side_right.start()
    on_right.wait_recv()
    side_a = send(half(far, 0), half(far, 0), pair(7), c=other)
    side_a.start()
    on_left.wait_recv()
    side_b = send(half(far, 1), half(far, 1), pair(8), c=other)
    side_b.start()
    first[2].wait_recv()
    for copy in (side_left, side_right, side_a, side_b, *overs, *grads_z):
        copy.wait_recv()
    for copy in (
        *first, on_right, on_left, side_left, side_right, side_a, side_b,
        *stage_y, *stage_z, *overs, *grads_y, *grads_z,
    ):
        copy.wait_send()
    for copy in (*keep, keep_o, keep_z):
        copy.wait()


def gather_rows(main, over, flag, band):
    dma = pltpu.SemaphoreType.DMA
    return pl.pallas_call(
        gather_kernel,
        in_specs=[ANY, ANY, VM, ANY],
        out_specs=[ANY, ANY, VM, ANY, ANY],
        out_shape=[
            jax.ShapeDtypeStruct((NDP, MAIN, DG), BF),
            jax.ShapeDtypeStruct((NDP, 2, DG), BF),
            jax.ShapeDtypeStruct((8, 128), F32),
            jax.ShapeDtypeStruct((NY, NZ, 16, 512), BF),
            jax.ShapeDtypeStruct((NZ, NY, 16, 512), BF),
        ],
        scratch_shapes=[
            pltpu.VMEM((NY, 16, DG), BF),
            pltpu.VMEM((NZ, 2, DG), BF),
            pltpu.VMEM((NZ, 2, DG), BF),
            pltpu.VMEM((2, DG), BF),
            pltpu.VMEM((NY, 8, 128), F32),
            pltpu.VMEM((8, 128), F32),
            pltpu.VMEM((NZ, 8, 128), F32),
            dma((8,)),
            dma((9,)),
            dma((9,)),
            dma((3, NY)),
            dma((3, NY)),
            dma((3, NZ)),
            dma((3, NZ)),
            dma((NDP,)),
            dma((NDP,)),
        ],
        compiler_params=pltpu.CompilerParams(
            collective_id=0, has_side_effects=True, vmem_limit_bytes=VMEM_LIMIT
        ),
        name="gather_rows",
    )(main, over, flag, band)


def spread_kernel(slot_ref, pooled_ref, over_ref, am_ref, ao_ref, spot_ref, out_ref, att_ref, rows_ref):
    slot = slot_ref[...]
    rows = lax.broadcasted_iota(jnp.int32, (2 * MAIN, BYTES), 0)
    onehot = jnp.where(rows == slot, 1.0, 0.0)
    counts = jnp.broadcast_to(jnp.sum(onehot, axis=1, keepdims=True), (2 * MAIN, 128))
    low = onehot.astype(BF)
    byte_count = jnp.maximum(dot_t(low, counts.astype(BF))[:, 0:1], 1.0)
    rows_ref[0:MAIN, :] = pooled_ref[0:MAIN, :]
    for j in range(NY):
        for k in range(NZ):
            at = MAIN + j * 16 + k * 2
            rows_ref[at : at + 2, :] = over_ref[j, k]
    out_ref[0] = (dot_t(low, rows_ref[...]) / byte_count).astype(BF)

    edge = 2 * spot_ref[0:1, 0:1].astype(jnp.int32) + 2
    row = lax.broadcasted_iota(jnp.int32, (66, 64), 0)
    col = lax.broadcasted_iota(jnp.int32, (66, 64), 1)
    keep = ((row < edge) & (col == row)) | ((row > edge + 1) & (col == row - 2))
    att = dot(jnp.where(keep, 1.0, 0.0).astype(BF), am_ref[0].reshape(64, 512))
    row = lax.broadcasted_iota(jnp.int32, (66, 16), 0)
    col = lax.broadcasted_iota(jnp.int32, (66, 16), 1)
    keep = (col == row - edge) & (col < 2)
    extra = jnp.concatenate([ao_ref[0], jnp.zeros((8, 512), BF)], axis=0)
    att = att + dot(jnp.where(keep, 1.0, 0.0).astype(BF), extra)
    att_ref[0] = att.astype(BF)


def spread(slot, pooled, over, am, ao, spot):
    steps = 4
    width = DG // steps
    return pl.pallas_call(
        spread_kernel,
        grid=(steps,),
        in_specs=[
            pl.BlockSpec((1, BYTES), lambda i: (0, 0)),
            pl.BlockSpec((72, width), lambda i: (0, i)),
            pl.BlockSpec((NY, NZ, 2, width), lambda i: (0, 0, 0, i)),
            pl.BlockSpec((1, NZ, 8, 512), lambda i: (i, 0, 0, 0)),
            pl.BlockSpec((1, 8, 512), lambda i: (i, 0, 0)),
            pl.BlockSpec((8, 128), lambda i: (0, 0)),
        ],
        out_specs=[
            pl.BlockSpec((1, BYTES, width), lambda i: (0, 0, i)),
            pl.BlockSpec((1, 66, 512), lambda i: (0, 0, i)),
        ],
        out_shape=[
            jax.ShapeDtypeStruct((1, BYTES, DG), BF),
            jax.ShapeDtypeStruct((1, 66, 2048), BF),
        ],
        scratch_shapes=[pltpu.VMEM((2 * MAIN, width), BF)],
        name="spread",
    )(slot, pooled, over, am, ao, spot)


ROWS = 72
OVER = 2


def project_kernel(main_ref, over_ref, weight_ref, out_ref, acc, acc_over, over_rows):
    step = pl.program_id(0)

    @pl.when(step == 0)
    def _():
        acc[...] = jnp.zeros_like(acc)
        acc_over[...] = jnp.zeros_like(acc_over)

    for n in range(NDP):
        over_rows[2 * n : 2 * n + 2, :] = over_ref[n]
    weight = weight_ref[...]
    acc[...] += dot(main_ref[...].reshape(NDP * MAIN, weight.shape[0]), weight)
    acc_over[...] += dot(over_rows[...], weight)

    @pl.when(step == pl.num_programs(0) - 1)
    def _():
        total = acc[...].astype(BF)
        extra = acc_over[...].astype(BF)
        for n in range(NDP):
            out_ref[n, 0:MAIN, :] = total[MAIN * n : MAIN * (n + 1)]
            out_ref[n, MAIN:ROWS, :] = jnp.zeros((ROWS - MAIN, COLS), BF)
            out_ref[n, MAIN : MAIN + 2, :] = extra[2 * n : 2 * n + 2]


def project(all_main, all_over, weight):
    steps = 4
    depth = DG // steps
    return pl.pallas_call(
        project_kernel,
        grid=(steps,),
        in_specs=[
            pl.BlockSpec((NDP, MAIN, depth), lambda i: (0, 0, i)),
            pl.BlockSpec((NDP, 2, depth), lambda i: (0, 0, i)),
            pl.BlockSpec((depth, COLS), lambda i: (i, 0)),
        ],
        out_specs=pl.BlockSpec((NDP, ROWS, COLS), lambda i: (0, 0, 0)),
        out_shape=jax.ShapeDtypeStruct((NDP, ROWS, COLS), BF),
        scratch_shapes=[
            pltpu.VMEM((NDP * MAIN, COLS), F32),
            pltpu.VMEM((16, COLS), F32),
            pltpu.VMEM((16, depth), BF),
        ],
        compiler_params=pltpu.CompilerParams(vmem_limit_bytes=VMEM_LIMIT),
        name="project",
    )(all_main, all_over, weight)


def lanes(i):
    return pl.ds(pl.multiple_of(i * HEAD, HEAD), HEAD)


def heads_kernel(proj, heads, kv, local, hs, hr, rs, rr, ls, lr):
    z, y, x, c = here()
    n = x * 2 + c
    up, down = lax.rem(z + 1, NZ), lax.rem(z + NZ - 1, NZ)
    peers = []
    for j in range(NDP * NY):
        if j:
            p, q = lax.rem(n + j // NY, NDP), lax.rem(y + j, NY)
            peers.append({"y": q, "x": p // 2, "c": lax.rem(p, 2)})
    greet(peers + [{"z": up}, {"z": down}])

    def plan(j, i):
        p = lax.rem(n + j, NDP)
        head = n * 3 + i
        query = head < QUERY_HEADS
        slot = jnp.where(query, lax.rem(head, 4), head // 4)
        target = jnp.where(query, head // 4, lax.rem(head, 4))
        src = proj.at[p, :, i * HEAD : (i + 1) * HEAD]
        dst = heads.at[slot, y]
        there = send(
            src, dst, (hs.at[j, i], hr.at[slot, y]), y=target, x=p // 2, c=lax.rem(p, 2)
        )
        stay = pltpu.make_async_copy(src, dst, hr.at[slot, y])
        own = target == y
        return there, stay, own

    for i in (2, 1, 0):
        for j in range(1, NDP):
            plan(j, i)[0].start()
        there, stay, own = plan(0, i)

        @pl.when(own)
        def _():
            stay.start()

        @pl.when(jnp.logical_not(own))
        def _():
            there.start()

    def arrived(slot, k):
        pltpu.make_async_copy(heads.at[slot, k], heads.at[slot, k], hr.at[slot, k]).wait()

    ups, downs, keeps = [], [], []
    for t in range(1, 5):
        for i in range(2):
            if t == 1:
                for k in range(NY):
                    arrived(4 + i, k)
                keep = pltpu.make_async_copy(heads.at[4 + i], kv.at[i, z], local.at[i])
                keep.start()
                keeps.append(keep)
                above = below = heads.at[4 + i]
            else:
                ups[2 * (t - 2) + i].wait_recv()
                downs[2 * (t - 2) + i].wait_recv()
                above = kv.at[i, lax.rem(z + NZ - (t - 1), NZ)]
                below = kv.at[i, lax.rem(z + (t - 1), NZ)]
            copy = send(above, kv.at[i, lax.rem(z + NZ - (t - 1), NZ)], (rs.at[t - 1, i], rr.at[t - 1, i]), z=up)
            copy.start()
            ups.append(copy)
            if t < 4:
                copy = send(below, kv.at[i, lax.rem(z + (t - 1), NZ)], (ls.at[t - 1, i], lr.at[t - 1, i]), z=down)
                copy.start()
                downs.append(copy)
    for slot in range(4):
        for k in range(NY):
            arrived(slot, k)
    for i in range(2):
        ups[6 + i].wait_recv()
    for copy in ups + downs:
        copy.wait_send()
    for copy in keeps:
        copy.wait()
    for i in range(3):
        for j in range(1, NDP):
            plan(j, i)[0].wait_send()
        there, stay, own = plan(0, i)

        @pl.when(jnp.logical_not(own))
        def _():
            there.wait_send()


def to_heads(proj):
    dma = pltpu.SemaphoreType.DMA
    return pl.pallas_call(
        heads_kernel,
        in_specs=[ANY],
        out_specs=[ANY, ANY],
        out_shape=[
            jax.ShapeDtypeStruct((6, NY, ROWS, HEAD), BF),
            jax.ShapeDtypeStruct((2, NZ, NY, ROWS, HEAD), BF),
        ],
        scratch_shapes=[
            dma((2,)),
            dma((NDP, 3)),
            dma((6, NY)),
            dma((4, 2)),
            dma((4, 2)),
            dma((3, 2)),
            dma((3, 2)),
        ],
        compiler_params=pltpu.CompilerParams(collective_id=1, has_side_effects=True),
        name="to_heads",
    )(proj)


CHUNK = 352
QM = 256
QO = 32
KM = NS * MAIN


def attention_kernel(
    heads_ref, kv_ref, gy_ref, gz_ref, spot_ref, kidx_ref, qidx_ref, qoidx_ref,
    om_ref, oo_ref, dq_ref, dkv_ref,
    k_ref, v_ref, kt, vt, g_ref, qo_ref, go_ref, scores, dk, dv,
):
    chunks = PATCHES // CHUNK
    z = lax.axis_index("z")
    spot = spot_ref[0:1, 0:1].astype(jnp.int32)

    for i, ref in enumerate((k_ref, v_ref)):
        for k in range(NZ):
            ref[k * QM : (k + 1) * QM, :] = kv_ref[i, k, :, 0:MAIN, :].reshape(QM, HEAD)
            for j in range(NY):
                at = KM + 2 * (k * NY + j)
                ref[at : at + 2, :] = kv_ref[i, k, j, MAIN : MAIN + 2, :]
    kt[...] = k_ref[...].astype(F32).T.astype(BF)
    vt[...] = v_ref[...].astype(F32).T.astype(BF)
    dk[...] = jnp.zeros_like(dk)
    dv[...] = jnp.zeros_like(dv)

    row = lax.broadcasted_iota(jnp.int32, (QM, 512), 0)
    col = lax.broadcasted_iota(jnp.int32, (QM, 512), 1)
    late = jnp.where(z * NY + (row >> 6) > spot, 2, 0)
    pick = jnp.where(col == (row & 31) * 16 + (row >> 5) + late, 1.0, 0.0).astype(BF)
    g_ref[...] = dot(pick, gz_ref[...].reshape(512, 512)).astype(BF)
    row = lax.broadcasted_iota(jnp.int32, (16, 512), 0)
    col = lax.broadcasted_iota(jnp.int32, (16, 512), 1)
    group = 2 * spot + 2 + (row & 1)
    band = jnp.minimum(group >> 3, NZ - 1)
    pick = jnp.where(
        (col == (row >> 1) * 128 + band * 16 + group - 8 * band) & (row < 8), 1.0, 0.0
    ).astype(BF)
    extra = dot(pick, gy_ref[...].reshape(512, 512)).astype(BF)
    for h in range(4):
        go_ref[8 * h : 8 * h + 8, :] = extra[0:8, HEAD * h : HEAD * (h + 1)]
        for j in range(NY):
            qo_ref[8 * h + 2 * j : 8 * h + 2 * j + 2, :] = heads_ref[h, j, MAIN : MAIN + 2, :]

    def span(c):
        return pl.ds(pl.multiple_of(c * CHUNK, 32), CHUNK)

    def block(q, g, qidx, width):
        qt = q.astype(F32).T.astype(BF)
        gt32 = g.astype(F32).T
        gt = gt32.astype(BF)

        peak = jnp.full((1, width), -jnp.inf, F32)
        for c in range(chunks):
            at = span(c)
            s = dot(k_ref[at, :], qt) * FACTOR
            s = jnp.where(kidx_ref[at, :] <= qidx, s, -jnp.inf)
            scores[at, :width] = s
            peak = jnp.maximum(peak, jnp.max(s, axis=0, keepdims=True))
        total = jnp.zeros((1, width), F32)
        for c in range(chunks):
            at = span(c)
            p = jnp.exp(scores[at, :width] - peak)
            scores[at, :width] = p
            total = total + jnp.sum(p, axis=0, keepdims=True)
        inverse = 1.0 / total
        out_t = jnp.zeros((HEAD, width), F32)
        for c in range(chunks):
            at = span(c)
            a = scores[at, :width] * inverse
            scores[at, :width] = a
            low = a.astype(BF)
            out_t = out_t + dot(vt[:, c * CHUNK : (c + 1) * CHUNK], low)
            dv[at, :] += dot(low, g)
        delta = jnp.sum(gt32 * out_t, axis=0, keepdims=True)
        dq_t = jnp.zeros((HEAD, width), F32)
        for c in range(chunks):
            at = span(c)
            da = dot(v_ref[at, :], gt)
            ds = (scores[at, :width] * (da - delta)).astype(BF)
            dq_t = dq_t + dot(kt[:, c * CHUNK : (c + 1) * CHUNK], ds)
            dk[at, :] += dot(ds, q)
        return out_t, (dq_t * FACTOR).T.astype(BF)

    row = lax.broadcasted_iota(jnp.int32, (QM, QM), 0)
    col = lax.broadcasted_iota(jnp.int32, (QM, QM), 1)
    turn = jnp.where(col == (row & 7) * 32 + (row >> 3), 1.0, 0.0).astype(BF)

    @pl.loop(0, 4)
    def _(h):
        q = heads_ref[h, :, 0:MAIN, :].reshape(QM, HEAD)
        out_t, dq = block(q, g_ref[:, lanes(h)], qidx_ref[...], QM)
        moved = lax.dot_general(
            turn, out_t.astype(BF), (((1,), (1,)), ((), ())), preferred_element_type=F32
        )
        om_ref[:, :, lanes(h)] = moved.astype(BF).reshape(NS, 8, HEAD)
        dq_ref[h, :, 0:MAIN, :] = dq.reshape(NY, MAIN, HEAD)

    out_t, dq = block(qo_ref[...], go_ref[...], qoidx_ref[...], QO)
    out = out_t.T.astype(BF)
    oo_ref[...] = jnp.zeros_like(oo_ref)
    dq_ref[:, :, MAIN:ROWS, :] = jnp.zeros((4, NY, ROWS - MAIN, HEAD), BF)
    for h in range(4):
        for j in range(NY):
            at = 8 * h + 2 * j
            oo_ref[j, 0:2, HEAD * h : HEAD * (h + 1)] = out[at : at + 2]
            dq_ref[h, j, MAIN : MAIN + 2, :] = dq[at : at + 2]
    for i, (ref, scale) in enumerate(((dk, FACTOR), (dv, 1.0))):
        for k in range(NZ):
            block_rows = (ref[k * QM : (k + 1) * QM, :] * scale).astype(BF)
            dkv_ref[i, k, :, 0:MAIN, :] = block_rows.reshape(NY, MAIN, HEAD)
        extra = (ref[KM:PATCHES, :] * scale).astype(BF)
        dkv_ref[i, :, :, MAIN:ROWS, :] = jnp.zeros((NZ, NY, ROWS - MAIN, HEAD), BF)
        for k in range(NZ):
            for j in range(NY):
                at = 2 * (k * NY + j)
                dkv_ref[i, k, j, MAIN : MAIN + 2, :] = extra[at : at + 2]


def attention(heads, kv, gy, gz, spot, kidx, qidx, qoidx):
    return pl.pallas_call(
        attention_kernel,
        in_specs=[VM] * 8,
        out_specs=[VM] * 4,
        out_shape=[
            jax.ShapeDtypeStruct((NS, 8, 512), BF),
            jax.ShapeDtypeStruct((NY, 8, 512), BF),
            jax.ShapeDtypeStruct((4, NY, ROWS, HEAD), BF),
            jax.ShapeDtypeStruct((2, NZ, NY, ROWS, HEAD), BF),
        ],
        scratch_shapes=[
            pltpu.VMEM((PATCHES, HEAD), BF),
            pltpu.VMEM((PATCHES, HEAD), BF),
            pltpu.VMEM((HEAD, PATCHES), BF),
            pltpu.VMEM((HEAD, PATCHES), BF),
            pltpu.VMEM((QM, 512), BF),
            pltpu.VMEM((QO, HEAD), BF),
            pltpu.VMEM((QO, HEAD), BF),
            pltpu.VMEM((PATCHES, QM), F32),
            pltpu.VMEM((PATCHES, HEAD), F32),
            pltpu.VMEM((PATCHES, HEAD), F32),
        ],
        compiler_params=pltpu.CompilerParams(vmem_limit_bytes=VMEM_LIMIT),
        name="attention",
    )(heads, kv, gy, gz, spot, kidx, qidx, qoidx)


def add(*parts):
    total = parts[0].astype(F32)
    for part in parts[1:]:
        total = total + part.astype(F32)
    return total.astype(BF)


def columns_kernel(
    dq, dkv, cols, ubuf, usum, dbuf, dsum, red, hs, hr, rs, rr, ls, lr
):
    z, y, x, c = here()
    n = x * 2 + c
    up, down = lax.rem(z + 1, NZ), lax.rem(z + NZ - 1, NZ)
    peers = []
    for j in range(1, NDP * NY):
        p, q = lax.rem(n + j // NY, NDP), lax.rem(y + j, NY)
        peers.append({"y": q, "x": p // 2, "c": lax.rem(p, 2)})
    greet(peers + [{"z": up}, {"z": down}])

    def plan(slot, j):
        k = lax.rem(y + j, NY)
        head = y * 4 + slot if slot < 4 else slot * 4 + y
        d, i = head // 3, lax.rem(head, 3)
        src = dq.at[slot, k] if slot < 4 else red.at[slot - 4, k]
        dst = cols.at[n, :, lanes(i)]
        there = lambda: send(
            src, dst, (hs.at[slot, j], hr.at[n, i]), y=k, x=d // 2, c=lax.rem(d, 2)
        )
        stay = lambda: pltpu.make_async_copy(src, dst, hr.at[n, i])
        return there, stay, d == n

    def start(slot):
        for j in range(1, NY):
            plan(slot, j)[0]().start()
        there, stay, own = plan(slot, 0)

        @pl.when(own)
        def _():
            stay().start()

        @pl.when(jnp.logical_not(own))
        def _():
            there().start()

    def sent(slot):
        for j in range(1, NY):
            plan(slot, j)[0]().wait_send()
        there, _, own = plan(slot, 0)

        @pl.when(jnp.logical_not(own))
        def _():
            there().wait_send()

    def at(k):
        return lax.rem(z + k, NZ)

    ups, downs = {}, {}
    for t in range(1, 5):
        for i in range(2):
            if t == 1:
                above, below = dkv.at[i, at(4)], dkv.at[i, at(5)]
            else:
                ups[t - 1, i].wait_recv()
                usum[i, t - 2] = add(ubuf[i, t - 2], dkv[i, at(5 - t)])
                above = usum.at[i, t - 2]
                if t < 4:
                    downs[t - 1, i].wait_recv()
                    dsum[i, t - 2] = add(dbuf[i, t - 2], dkv[i, at(4 + t)])
                    below = dsum.at[i, t - 2]
            ups[t, i] = send(above, ubuf.at[i, t - 1], (rs.at[t - 1, i], rr.at[t - 1, i]), z=up)
            ups[t, i].start()
            if t < 4:
                downs[t, i] = send(
                    below, dbuf.at[i, t - 1], (ls.at[t - 1, i], lr.at[t - 1, i]), z=down
                )
                downs[t, i].start()
        if t == 1:
            for slot in range(4):
                start(slot)
    for i in range(2):
        downs[3, i].wait_recv()
        ups[4, i].wait_recv()
        red[i] = add(ubuf[i, 3], dbuf[i, 2], dkv[i, z])
        start(4 + i)
    for p in range(NDP):
        for i in range(3):
            block = cols.at[p, :, i * HEAD : (i + 1) * HEAD]
            pltpu.make_async_copy(block, block, hr.at[p, i]).wait()
    for copy in (*ups.values(), *downs.values()):
        copy.wait_send()
    for slot in range(6):
        sent(slot)


def to_columns(dq, dkv):
    dma = pltpu.SemaphoreType.DMA
    part = (NY, ROWS, HEAD)
    return pl.pallas_call(
        columns_kernel,
        in_specs=[VM, VM],
        out_specs=ANY,
        out_shape=jax.ShapeDtypeStruct((NDP, ROWS, COLS), BF),
        scratch_shapes=[
            pltpu.VMEM((2, 4, *part), BF),
            pltpu.VMEM((2, 3, *part), BF),
            pltpu.VMEM((2, 3, *part), BF),
            pltpu.VMEM((2, 2, *part), BF),
            pltpu.VMEM((2, *part), BF),
            dma((6, NY)),
            dma((NDP, 3)),
            dma((4, 2)),
            dma((4, 2)),
            dma((3, 2)),
            dma((3, 2)),
        ],
        compiler_params=pltpu.CompilerParams(
            collective_id=2, has_side_effects=True, vmem_limit_bytes=VMEM_LIMIT
        ),
        name="to_columns",
    )(dq, dkv)


def products_kernel(main_ref, over_ref, cols_ref, weight_ref, part_ref, back_ref, cm, co, over_rows):
    @pl.when(pl.program_id(0) == 0)
    def _():
        for n in range(NDP):
            cm[MAIN * n : MAIN * (n + 1), :] = cols_ref[n, 0:MAIN, :]
            co[2 * n : 2 * n + 2, :] = cols_ref[n, MAIN : MAIN + 2, :]

    width = weight_ref.shape[0]
    for n in range(NDP):
        over_rows[2 * n : 2 * n + 2, :] = over_ref[n]
    part = dot_t(main_ref[...].reshape(NDP * MAIN, width), cm[...]) + dot_t(over_rows[...], co[...])
    part_ref[0] = part.astype(BF).reshape(NY, HEAD, COLS)
    turn = (((1,), (1,)), ((), ()))
    back = lax.dot_general(cm[...], weight_ref[...], turn, preferred_element_type=F32)
    extra = lax.dot_general(co[...], weight_ref[...], turn, preferred_element_type=F32)
    back = back.astype(BF)
    extra = extra.astype(BF)
    for n in range(NDP):
        back_ref[n, 0:MAIN, :] = back[MAIN * n : MAIN * (n + 1)]
        back_ref[n, MAIN:ROWS, :] = jnp.zeros((ROWS - MAIN, width), BF)
        back_ref[n, MAIN : MAIN + 2, :] = extra[2 * n : 2 * n + 2]


def products(all_main, all_over, cols, weight):
    steps = NZ
    width = DG // steps
    return pl.pallas_call(
        products_kernel,
        grid=(steps,),
        in_specs=[
            pl.BlockSpec((NDP, MAIN, width), lambda i: (0, 0, i)),
            pl.BlockSpec((NDP, 2, width), lambda i: (0, 0, i)),
            pl.BlockSpec((NDP, ROWS, COLS), lambda i: (0, 0, 0)),
            pl.BlockSpec((width, COLS), lambda i: (i, 0)),
        ],
        out_specs=[
            pl.BlockSpec((1, NY, HEAD, COLS), lambda i: (i, 0, 0, 0)),
            pl.BlockSpec((NDP, ROWS, width), lambda i: (0, 0, i)),
        ],
        out_shape=[
            jax.ShapeDtypeStruct((NZ, NY, HEAD, COLS), BF),
            jax.ShapeDtypeStruct((NDP, ROWS, DG), BF),
        ],
        scratch_shapes=[
            pltpu.VMEM((NDP * MAIN, COLS), BF),
            pltpu.VMEM((16, COLS), BF),
            pltpu.VMEM((16, width), BF),
        ],
        compiler_params=pltpu.CompilerParams(vmem_limit_bytes=VMEM_LIMIT),
        name="products",
    )(all_main, all_over, cols, weight)


def sums_kernel(
    back, w, om, oo,
    pooled, over_all, wgrad, am, ao,
    own, sib, chip, xa, xb, xr, xl, sxa, sxb,
    ya, yb, yr, yl, sa, sb, wy, ubuf, usum, dbuf, dsum, omz, ov, oz,
    local, cs, cr, xs, xrv, ws, wr, us, ur, ds, dr, zs, zr, os_, or_,
):
    z, y, x, c = here()
    right, left, far = lax.rem(x + 1, NX), lax.rem(x + 3, NX), lax.rem(x + 2, NX)
    yn, yp, yf = lax.rem(y + 1, NY), lax.rem(y + 3, NY), lax.rem(y + 2, NY)
    up, down = lax.rem(z + 1, NZ), lax.rem(z + NZ - 1, NZ)
    ys_at = [lax.rem(y + j, NY) for j in range(NY)]
    zs_at = [lax.rem(z + j, NZ) for j in range(NZ)]
    greet(
        [{"y": ys_at[j]} for j in range(1, NY)]
        + [{"z": zs_at[j]} for j in range(1, NZ)]
        + [{"x": right}, {"x": left}, {"c": 1 - c}]
    )
    copies = []

    def go(src, dst, pair, **device):
        copy = send(src, dst, pair, **device)
        copy.start()
        copies.append(copy)
        return copy

    order = (far, right, left, x)
    halves = [
        go(back.at[p * 2 + 1 - c], sib.at[p], (cs.at[k], cr.at[k]), c=1 - c)
        for k, p in enumerate(order)
    ]
    loads = [
        pltpu.make_async_copy(back.at[p * 2 + c], own.at[p], local.at[k])
        for k, p in enumerate(order)
    ]
    for copy in loads:
        copy.start()

    lo, hi = pl.ds(0, 4), pl.ds(4, 4)
    w_a = go(w.at[lo, yf], ya, (ws.at[0], wr.at[0]), y=yn)
    w_b = go(w.at[hi, yf], yb, (ws.at[1], wr.at[1]), y=yp)
    w_hi = go(w.at[hi, yn], yr.at[hi], (ws.at[2], wr.at[2]), y=yn)
    w_lo = go(w.at[lo, yp], yl.at[lo], (ws.at[3], wr.at[3]), y=yp)

    rows_z = [
        go(om.at[zs_at[j]], omz.at[z], (zs.at[0, j], zr.at[0, j]), z=zs_at[j])
        for j in range(1, NZ)
    ]
    stay_z = pltpu.make_async_copy(om.at[z], omz.at[z], local.at[4])
    stay_z.start()

    first, second = pl.ds(0, DG // 2), pl.ds(DG // 2, DG // 2)
    for k, p in enumerate(order):
        loads[k].wait()
        halves[k].wait_recv()
        chip[p] = add(own[p], sib[p])
        if k == 0:
            x_a = go(chip.at[p, :, first], xa, (xs.at[0], xrv.at[0]), x=right)
            x_b = go(chip.at[p, :, second], xb, (xs.at[1], xrv.at[1]), x=left)
        if k == 1:
            x_hi = go(chip.at[p, :, second], xr.at[:, second], (xs.at[2], xrv.at[2]), x=right)
        if k == 2:
            x_lo = go(chip.at[p, :, first], xl.at[:, first], (xs.at[3], xrv.at[3]), x=left)

    w_a.wait_recv()
    sa[...] = add(ya[...], w[lo, yn])
    w_lo2 = go(sa, yr.at[lo], (ws.at[4], wr.at[4]), y=yn)
    w_b.wait_recv()
    sb[...] = add(yb[...], w[hi, yp])
    w_hi2 = go(sb, yl.at[hi], (ws.at[5], wr.at[5]), y=yp)
    x_a.wait_recv()
    sxa[...] = add(xa[...], chip[right, :, first])
    x_lo2 = go(sxa, xr.at[:, first], (xs.at[4], xrv.at[4]), x=right)
    x_b.wait_recv()
    sxb[...] = add(xb[...], chip[left, :, second])
    x_hi2 = go(sxb, xl.at[:, second], (xs.at[5], xrv.at[5]), x=left)

    for copy in rows_z:
        copy.wait_recv()
    stay_z.wait()
    rows_y = []
    for j in range(1, NY):
        k = ys_at[j]
        rows_y.append(go(omz.at[:, k], am.at[y], (os_.at[0, j], or_.at[0, j]), y=k))
        rows_y.append(go(oo.at[k], ao.at[y], (os_.at[1, j], or_.at[1, j]), y=k))
    stay_y = [
        pltpu.make_async_copy(omz.at[:, y], am.at[y], local.at[5]),
        pltpu.make_async_copy(oo.at[y], ao.at[y], local.at[6]),
    ]
    for copy in stay_y:
        copy.start()

    for copy in (x_hi, x_lo, x_lo2, x_hi2):
        copy.wait_recv()
    pooled[...] = add(chip[x], xr[...], xl[...])
    ov[...] = pooled[MAIN : MAIN + 2, :]
    over_z = [
        go(ov, oz.at[z], (zs.at[1, j], zr.at[1, j]), z=zs_at[j]) for j in range(1, NZ)
    ]
    keep_z = pltpu.make_async_copy(ov, oz.at[z], local.at[7])
    keep_z.start()

    for copy in (w_hi, w_lo, w_lo2, w_hi2):
        copy.wait_recv()
    wy[...] = add(w[:, y], yr[...], yl[...])

    def at(k):
        return lax.rem(z + k, NZ)

    ups, downs = {}, {}
    over_y = []
    for t in range(1, 5):
        if t == 1:
            above, below = wy.at[at(4)], wy.at[at(5)]
        else:
            ups[t - 1].wait_recv()
            usum[t - 2] = add(ubuf[t - 2], wy[at(5 - t)])
            above = usum.at[t - 2]
            if t < 4:
                downs[t - 1].wait_recv()
                dsum[t - 2] = add(dbuf[t - 2], wy[at(4 + t)])
                below = dsum.at[t - 2]
        ups[t] = go(above, ubuf.at[t - 1], (us.at[t - 1], ur.at[t - 1]), z=up)
        if t < 4:
            downs[t] = go(below, dbuf.at[t - 1], (ds.at[t - 1], dr.at[t - 1]), z=down)
        if t == 1:
            for copy in over_z:
                copy.wait_recv()
            keep_z.wait()
            for j in range(1, NY):
                over_y.append(
                    go(oz, over_all.at[y], (os_.at[2, j], or_.at[2, j]), y=ys_at[j])
                )
            keep_y = pltpu.make_async_copy(oz, over_all.at[y], local.at[8])
            keep_y.start()
    downs[3].wait_recv()
    ups[4].wait_recv()
    wgrad[...] = ubuf[3].astype(F32) + dbuf[2].astype(F32) + wy[z].astype(F32)
    for copy in (*over_y, *rows_y):
        copy.wait_recv()
    for copy in copies:
        copy.wait_send()
    for copy in (*stay_y, keep_y):
        copy.wait()


def sums(back, part, om, oo):
    dma = pltpu.SemaphoreType.DMA
    rows = (ROWS, DG)
    half = (ROWS, DG // 2)
    block = (HEAD, COLS)
    return pl.pallas_call(
        sums_kernel,
        in_specs=[ANY, VM, ANY, ANY],
        out_specs=[VM, ANY, VM, ANY, ANY],
        out_shape=[
            jax.ShapeDtypeStruct(rows, BF),
            jax.ShapeDtypeStruct((NY, NZ, 2, DG), BF),
            jax.ShapeDtypeStruct(block, F32),
            jax.ShapeDtypeStruct((NY, NZ, 8, 512), BF),
            jax.ShapeDtypeStruct((NY, 8, 512), BF),
        ],
        scratch_shapes=[
            *[pltpu.VMEM((NX, *rows), BF)] * 3,
            *[pltpu.VMEM(half, BF)] * 2,
            *[pltpu.VMEM(rows, BF)] * 2,
            *[pltpu.VMEM(half, BF)] * 2,
            *[pltpu.VMEM((4, *block), BF)] * 2,
            *[pltpu.VMEM((8, *block), BF)] * 2,
            *[pltpu.VMEM((4, *block), BF)] * 2,
            pltpu.VMEM((8, *block), BF),
            pltpu.VMEM((4, *block), BF),
            pltpu.VMEM((3, *block), BF),
            pltpu.VMEM((3, *block), BF),
            pltpu.VMEM((2, *block), BF),
            pltpu.VMEM((NZ, NY, 8, 512), BF),
            pltpu.VMEM((2, DG), BF),
            pltpu.VMEM((NZ, 2, DG), BF),
            dma((9,)),
            dma((4,)),
            dma((4,)),
            dma((6,)),
            dma((6,)),
            dma((6,)),
            dma((6,)),
            dma((4,)),
            dma((4,)),
            dma((3,)),
            dma((3,)),
            dma((2, NZ)),
            dma((2, NZ)),
            dma((3, NY)),
            dma((3, NY)),
        ],
        compiler_params=pltpu.CompilerParams(
            collective_id=3, has_side_effects=True, vmem_limit_bytes=VMEM_LIMIT
        ),
        name="sums",
    )(back, part, om, oo)


def body(byte_states, byte_patch, patch_owner, qkv_weight, attention_output_gradient):
    z, y = lax.axis_index("z"), lax.axis_index("y")
    s = z * NY + y
    main, over, slot, flag, band = pool(
        byte_patch, patch_owner, byte_states, attention_output_gradient
    )
    all_main, all_over, found, grad_y, grad_z = gather_rows(main, over, flag, band)
    spot = found[0, 0].astype(jnp.int32)

    owners = patch_owner[0].reshape(66, 32)
    who = jnp.arange(32, dtype=jnp.int32)
    place = jnp.sum(
        jnp.where(owners[:, :, None] == who[None, None, :], who[None, :, None], 0), axis=1
    )
    index = place + 32 * jnp.arange(66, dtype=jnp.int32)[:, None]
    flat = index.reshape(-1)
    row = jnp.arange(2048, dtype=jnp.int32)
    main_index = jnp.where(row < MAIN * (spot + 1), flat[:2048], flat[64:])
    over_index = lax.dynamic_slice_in_dim(index, 2 * spot + 2, 2, 0).T.reshape(-1)
    key_index = jnp.concatenate([main_index, over_index])
    query_index = lax.dynamic_slice_in_dim(main_index, z * QM, QM)
    query_over_index = lax.dynamic_slice_in_dim(over_index, z * 8, 8)

    proj = project(all_main, all_over, qkv_weight)
    heads, kv = to_heads(proj)
    om, oo, dq, dkv = attention(
        heads, kv, grad_y, grad_z, found,
        key_index[:, None], query_index[None], jnp.tile(query_over_index, 4)[None],
    )

    cols = to_columns(dq, dkv)
    part, back = products(all_main, all_over, cols, qkv_weight)
    pooled, over_back, weight_grad, am, ao = sums(back, part, om.reshape(NZ, NY, 8, 512), oo)
    state_grad, att = spread(slot, pooled, over_back, am, ao, found)
    return att, state_grad, weight_grad


def solution(mesh):
    finer = Mesh(mesh.devices.reshape(NZ, NY, NX, NC), ("z", "y", "x", "c"))
    placed = (P(DP, SEQ, None), P(DP, SEQ), P(DP, None), P(None, DP), P(DP, SEQ, None))
    return jax.shard_map(
        body,
        mesh=finer,
        in_specs=placed,
        out_specs=(P(DP, SEQ, None), P(DP, SEQ, None), P(SEQ, DP)),
        check_vma=False,
    )
```

```python
import functools

import jax
import jax.numpy as jnp
from jax import lax
from jax.experimental import pallas as pl
from jax.experimental.pallas import tpu as pltpu
from jax.sharding import Mesh
from jax.sharding import PartitionSpec as P

QUERY_HEADS = 16
KEY_VALUE_HEADS = 4
HEAD = 128
FACTOR = HEAD ** (-0.5)
NZ, NY, NX, NC = 8, 4, 4, 2
NS, NDP = NZ * NY, NX * NC
SEQ = ("z", "y")
DP = ("x", "c")
MAIN = 64
BYTES = 256
DG = 4096
PATCHES = 2112
COLS = 384
BF = jnp.bfloat16
F32 = jnp.float32
VMEM_LIMIT = 56 << 20


def dot(a, b):
    return jnp.dot(a, b, preferred_element_type=F32)


def dot_t(a, b):
    return lax.dot_general(a, b, (((0,), (0,)), ((), ())), preferred_element_type=F32)


def pool_kernel(
    ids_ref, owner_ref, states_ref, grad_ref,
    main_ref, over_ref, slot_ref, flag_ref, band_ref,
    onehot_ref,
):
    s = lax.axis_index("z") * NY + lax.axis_index("y")

    @pl.when(pl.program_id(0) == 0)
    def _():
        ids = ids_ref[...]
        first = jnp.min(ids, axis=1, keepdims=True)
        last = jnp.max(ids, axis=1, keepdims=True)
        group = (ids - first) >> 5
        patch = lax.broadcasted_iota(jnp.int32, (PATCHES, BYTES), 0)
        hit = jnp.where(patch == ids, 1.0, 0.0).astype(BF)
        owner = jnp.broadcast_to(owner_ref[...].astype(F32), (16, PATCHES)).astype(BF)
        byte_owner = dot(owner, hit)[0:1].astype(jnp.int32)
        over = MAIN + (byte_owner & 3) * 16 + (byte_owner >> 2) * 2 + (group - 2)
        slot = jnp.where(group < 2, group * 32 + byte_owner, over)
        slot_ref[...] = slot
        rows = lax.broadcasted_iota(jnp.int32, (2 * MAIN, BYTES), 0)
        onehot_ref[...] = jnp.where(rows == slot, 1.0, 0.0)
        spike = jnp.where(last - first >= MAIN, s.astype(F32), 0.0)
        flag_ref[...] = jnp.broadcast_to(spike, (8, 128))

    onehot = onehot_ref[...]
    counts = jnp.maximum(jnp.sum(onehot, axis=1, keepdims=True), 1.0)
    pooled = (dot(onehot.astype(BF), states_ref[0]) / counts).astype(BF)
    main_ref[...] = pooled[:MAIN]
    over_ref[...] = pooled[MAIN:].reshape(NY, 16, pooled.shape[1])
    grad = grad_ref[0]
    for z in range(NZ - 1):
        band_ref[z] = grad[8 * z : 8 * z + 16]
    band_ref[NZ - 1] = jnp.zeros_like(band_ref[NZ - 1])
    band_ref[NZ - 1, 0:10, :] = grad[56:66]


def pool(byte_patch, patch_owner, byte_states, grad):
    steps = 4
    width = DG // steps
    return pl.pallas_call(
        pool_kernel,
        grid=(steps,),
        in_specs=[
            pl.BlockSpec((1, BYTES), lambda i: (0, 0)),
            pl.BlockSpec((1, PATCHES), lambda i: (0, 0)),
            pl.BlockSpec((1, BYTES, width), lambda i: (0, 0, i)),
            pl.BlockSpec((1, 66, 512), lambda i: (0, 0, i)),
        ],
        out_specs=[
            pl.BlockSpec((MAIN, width), lambda i: (0, i)),
            pl.BlockSpec((NY, 16, width), lambda i: (0, 0, i)),
            pl.BlockSpec((1, BYTES), lambda i: (0, 0)),
            pl.BlockSpec((8, 128), lambda i: (0, 0)),
            pl.BlockSpec((NZ, 16, 512), lambda i: (0, 0, i)),
        ],
        out_shape=[
            jax.ShapeDtypeStruct((MAIN, DG), BF),
            jax.ShapeDtypeStruct((NY, 16, DG), BF),
            jax.ShapeDtypeStruct((1, BYTES), jnp.int32),
            jax.ShapeDtypeStruct((8, 128), F32),
            jax.ShapeDtypeStruct((NZ, 16, 2048), BF),
        ],
        scratch_shapes=[pltpu.VMEM((2 * MAIN, BYTES), F32)],
        name="pool",
    )(byte_patch, patch_owner, byte_states, grad)


MESH = pl.DeviceIdType.MESH
ANY = pl.BlockSpec(memory_space=pl.ANY)
VM = pl.BlockSpec(memory_space=pltpu.VMEM)


def add(*parts):
    total = parts[0].astype(F32)
    for part in parts[1:]:
        total = total + part.astype(F32)
    return total.astype(BF)


def here():
    return [lax.axis_index(name) for name in ("z", "y", "x", "c")]


def send(src, dst, pair, **device):
    return pltpu.make_async_remote_copy(
        src_ref=src, dst_ref=dst, send_sem=pair[0], recv_sem=pair[1],
        device_id=device, device_id_type=MESH,
    )


def greet(devices):
    barrier = pltpu.get_barrier_semaphore()
    for device in devices:
        pl.semaphore_signal(barrier, inc=1, device_id=device, device_id_type=MESH)
    pl.semaphore_wait(barrier, len(devices))


def gather_kernel(
    main, over, flag, band, grad,
    all_main, all_over, spot, gy, gz,
    ybuf, zsrc, zbuf, mine, fy, fsum, fz, gband,
    local, main_s, main_r, ys, yr, zs, zr, os_, or_,
):
    z, y, x, c = here()
    n = x * 2 + c
    ys_at = [lax.rem(y + j, NY) for j in range(NY)]
    zs_at = [lax.rem(z + j, NZ) for j in range(NZ)]
    dp_at = [lax.rem(n + j, NDP) for j in range(NDP)]
    right, left, twin = lax.rem(x + 1, NX), lax.rem(x + 3, NX), 1 - c
    greet(
        [{"y": ys_at[j]} for j in range(1, NY)]
        + [{"z": zs_at[j]} for j in range(1, NZ)]
        + [{"x": p // 2, "c": lax.rem(p, 2)} for p in dp_at[1:]]
    )
    copies, stays = [], []

    def go(src, dst, pair, **device):
        copy = send(src, dst, pair, **device)
        copy.start()
        copies.append(copy)
        return copy

    def stay(src, dst):
        copy = pltpu.make_async_copy(src, dst, local.at[len(stays)])
        copy.start()
        stays.append(copy)
        return copy

    def half(block, i):
        return block.at[pl.ds(32 * i, 32), :]

    def pair(i):
        return main_s.at[i], main_r.at[i]

    def columns(h):
        return pl.ds(pl.multiple_of(h * 512, 512), 512)

    stage_y = []
    for j in range(1, NY):
        k = ys_at[j]
        stage_y.append(go(over.at[k], ybuf.at[y], (ys.at[0, j], yr.at[0, j]), y=k))
        stage_y.append(go(flag, fy.at[y], (ys.at[1, j], yr.at[1, j]), y=k))
    here_y = [stay(over.at[y], ybuf.at[y]), stay(flag, fy.at[y])]

    mine_out = all_main.at[n]
    to_right = go(main, mine_out, pair(1), x=right)
    to_left = go(main, mine_out, pair(2), x=left)
    to_other = go(main, mine_out, pair(0), c=twin)
    stay(main, mine_out)

    bands_z = [
        go(band.at[zs_at[j]], gband.at[z], (zs.at[2, j], zr.at[2, j]), z=zs_at[j])
        for j in range(1, NZ)
    ]
    here_band = stay(band.at[z], gband.at[z])

    for copy in stage_y:
        copy.wait_recv()
    for copy in here_y:
        copy.wait()
    rows = add(ybuf[0], ybuf[1], ybuf[2], ybuf[3])
    for k in range(NZ):
        zsrc[k] = rows[2 * k : 2 * k + 2]
    fsum[...] = fy[0] + fy[1] + fy[2] + fy[3]
    stage_z = []
    for j in range(1, NZ):
        k = zs_at[j]
        stage_z.append(go(zsrc.at[k], zbuf.at[z], (zs.at[0, j], zr.at[0, j]), z=k))
        stage_z.append(go(fsum, fz.at[z], (zs.at[1, j], zr.at[1, j]), z=k))
    here_z = [stay(zsrc.at[z], zbuf.at[z]), stay(fsum, fz.at[z])]
    grads_y = [
        go(grad.at[0, :, columns(ys_at[j])], gy.at[y], (ys.at[2, j], yr.at[2, j]), y=ys_at[j])
        for j in range(1, NY)
    ]
    stay(grad.at[0, :, columns(y)], gy.at[y])

    for copy in stage_z:
        copy.wait_recv()
    for copy in here_z:
        copy.wait()
    total = zbuf[0].astype(F32)
    found = fz[0]
    for k in range(1, NZ):
        total = total + zbuf[k].astype(F32)
        found = found + fz[k]
    mine[...] = total.astype(BF)
    spot[...] = found
    overs = [
        go(mine, all_over.at[n], (os_.at[j], or_.at[j]), x=dp_at[j] // 2, c=lax.rem(dp_at[j], 2))
        for j in range(1, NDP)
    ]
    stay(mine, all_over.at[n])

    from_left = all_main.at[left * 2 + c]
    from_right = all_main.at[right * 2 + c]
    far = all_main.at[lax.rem(x + 2, NX) * 2 + c]
    to_right.wait_recv()
    on_right = go(half(from_left, 0), half(from_left, 0), pair(3), x=right)
    side_left = go(from_left, from_left, pair(5), c=twin)
    to_left.wait_recv()
    on_left = go(half(from_right, 1), half(from_right, 1), pair(4), x=left)
    side_right = go(from_right, from_right, pair(6), c=twin)

    for copy in bands_z:
        copy.wait_recv()
    here_band.wait()
    bands_y = [
        go(gband.at[:, :, columns(ys_at[j])], gz.at[:, y], (ys.at[3, j], yr.at[3, j]), y=ys_at[j])
        for j in range(1, NY)
    ]
    stay(gband.at[:, :, columns(y)], gz.at[:, y])

    on_right.wait_recv()
    side_a = go(half(far, 0), half(far, 0), pair(7), c=twin)
    on_left.wait_recv()
    side_b = go(half(far, 1), half(far, 1), pair(8), c=twin)
    for copy in (to_other, side_left, side_right, side_a, side_b, *overs, *grads_y, *bands_y):
        copy.wait_recv()
    for copy in copies:
        copy.wait_send()
    for copy in stays:
        if not any(copy is other for other in (*here_y, *here_z, here_band)):
            copy.wait()


def gather_rows(main, over, flag, band, grad):
    dma = pltpu.SemaphoreType.DMA
    return pl.pallas_call(
        gather_kernel,
        in_specs=[ANY, ANY, VM, ANY, ANY],
        out_specs=[ANY, ANY, VM, ANY, ANY],
        out_shape=[
            jax.ShapeDtypeStruct((NDP, MAIN, DG), BF),
            jax.ShapeDtypeStruct((NDP, 2, DG), BF),
            jax.ShapeDtypeStruct((8, 128), F32),
            jax.ShapeDtypeStruct((NY, 66, 512), BF),
            jax.ShapeDtypeStruct((NZ, NY, 16, 512), BF),
        ],
        scratch_shapes=[
            pltpu.VMEM((NY, 16, DG), BF),
            pltpu.VMEM((NZ, 2, DG), BF),
            pltpu.VMEM((NZ, 2, DG), BF),
            pltpu.VMEM((2, DG), BF),
            pltpu.VMEM((NY, 8, 128), F32),
            pltpu.VMEM((8, 128), F32),
            pltpu.VMEM((NZ, 8, 128), F32),
            pltpu.VMEM((NZ, 16, 2048), BF),
            dma((9,)),
            dma((9,)),
            dma((9,)),
            dma((4, NY)),
            dma((4, NY)),
            dma((3, NZ)),
            dma((3, NZ)),
            dma((NDP,)),
            dma((NDP,)),
        ],
        compiler_params=pltpu.CompilerParams(
            collective_id=0, has_side_effects=True, vmem_limit_bytes=VMEM_LIMIT
        ),
        name="gather_rows",
    )(main, over, flag, band, grad)


def spread_kernel(
    slot_ref, pooled_ref, over_ref, am_ref, ao_ref, spot_ref, wide_ref,
    out_ref, att_ref, weight_ref,
    rows_ref,
):
    @pl.when(pl.program_id(0) == 0)
    def _():
        weight_ref[...] = wide_ref[...].T

    slot = slot_ref[...]
    rows = lax.broadcasted_iota(jnp.int32, (2 * MAIN, BYTES), 0)
    onehot = jnp.where(rows == slot, 1.0, 0.0)
    counts = jnp.broadcast_to(jnp.sum(onehot, axis=1, keepdims=True), (2 * MAIN, 128))
    low = onehot.astype(BF)
    byte_count = jnp.maximum(dot_t(low, counts.astype(BF))[:, 0:1], 1.0)
    rows_ref[0:MAIN, :] = pooled_ref[0:MAIN, :]
    for j in range(NY):
        for k in range(NZ):
            at = MAIN + j * 16 + k * 2
            rows_ref[at : at + 2, :] = over_ref[j, k]
    out_ref[0] = (dot_t(low, rows_ref[...]) / byte_count).astype(BF)

    edge = 2 * spot_ref[0:1, 0:1].astype(jnp.int32) + 2
    row = lax.broadcasted_iota(jnp.int32, (66, 64), 0)
    col = lax.broadcasted_iota(jnp.int32, (66, 64), 1)
    keep = ((row < edge) & (col == row)) | ((row > edge + 1) & (col == row - 2))
    att = dot(jnp.where(keep, 1.0, 0.0).astype(BF), am_ref[0].reshape(64, 512))
    row = lax.broadcasted_iota(jnp.int32, (66, 16), 0)
    col = lax.broadcasted_iota(jnp.int32, (66, 16), 1)
    keep = (col == row - edge) & (col < 2)
    extra = jnp.concatenate([ao_ref[0], jnp.zeros((8, 512), BF)], axis=0)
    att = att + dot(jnp.where(keep, 1.0, 0.0).astype(BF), extra)
    att_ref[0] = att.astype(BF)


def spread(slot, pooled, over, am, ao, spot, wide):
    steps = 4
    width = DG // steps
    return pl.pallas_call(
        spread_kernel,
        grid=(steps,),
        in_specs=[
            pl.BlockSpec((1, BYTES), lambda i: (0, 0)),
            pl.BlockSpec((MAIN, width), lambda i: (0, i)),
            pl.BlockSpec((NY, NZ, 2, width), lambda i: (0, 0, 0, i)),
            pl.BlockSpec((1, NZ, 8, 512), lambda i: (i, 0, 0, 0)),
            pl.BlockSpec((1, 8, 512), lambda i: (i, 0, 0)),
            pl.BlockSpec((8, 128), lambda i: (0, 0)),
            pl.BlockSpec((COLS, HEAD), lambda i: (0, 0)),
        ],
        out_specs=[
            pl.BlockSpec((1, BYTES, width), lambda i: (0, 0, i)),
            pl.BlockSpec((1, 66, 512), lambda i: (0, 0, i)),
            pl.BlockSpec((HEAD, COLS), lambda i: (0, 0)),
        ],
        out_shape=[
            jax.ShapeDtypeStruct((1, BYTES, DG), BF),
            jax.ShapeDtypeStruct((1, 66, 2048), BF),
            jax.ShapeDtypeStruct((HEAD, COLS), F32),
        ],
        scratch_shapes=[pltpu.VMEM((2 * MAIN, width), BF)],
        name="spread",
    )(slot, pooled, over, am, ao, spot, wide)


ROWS = 72
OVER = 2


def project_kernel(main_ref, over_ref, weight_ref, out_ref, acc, acc_over, over_rows):
    step = pl.program_id(0)

    @pl.when(step == 0)
    def _():
        acc[...] = jnp.zeros_like(acc)
        acc_over[...] = jnp.zeros_like(acc_over)

    for n in range(NDP):
        over_rows[2 * n : 2 * n + 2, :] = over_ref[n]
    weight = weight_ref[...]
    acc[...] += dot(main_ref[...].reshape(NDP * MAIN, weight.shape[0]), weight)
    acc_over[...] += dot(over_rows[...], weight)

    @pl.when(step == pl.num_programs(0) - 1)
    def _():
        total = acc[...].astype(BF)
        extra = acc_over[...].astype(BF)
        for n in range(NDP):
            out_ref[n, 0:MAIN, :] = total[MAIN * n : MAIN * (n + 1)]
            out_ref[n, MAIN:ROWS, :] = jnp.zeros((ROWS - MAIN, COLS), BF)
            out_ref[n, MAIN : MAIN + 2, :] = extra[2 * n : 2 * n + 2]


def project(all_main, all_over, weight):
    steps = 4
    depth = DG // steps
    return pl.pallas_call(
        project_kernel,
        grid=(steps,),
        in_specs=[
            pl.BlockSpec((NDP, MAIN, depth), lambda i: (0, 0, i)),
            pl.BlockSpec((NDP, 2, depth), lambda i: (0, 0, i)),
            pl.BlockSpec((depth, COLS), lambda i: (i, 0)),
        ],
        out_specs=pl.BlockSpec((NDP, ROWS, COLS), lambda i: (0, 0, 0)),
        out_shape=jax.ShapeDtypeStruct((NDP, ROWS, COLS), BF),
        scratch_shapes=[
            pltpu.VMEM((NDP * MAIN, COLS), F32),
            pltpu.VMEM((16, COLS), F32),
            pltpu.VMEM((16, depth), BF),
        ],
        compiler_params=pltpu.CompilerParams(vmem_limit_bytes=VMEM_LIMIT),
        name="project",
    )(all_main, all_over, weight)


def lanes(i):
    return pl.ds(pl.multiple_of(i * HEAD, HEAD), HEAD)


def heads_kernel(proj, heads, kv, local, hs, hr, rs, rr, ls, lr):
    z, y, x, c = here()
    n = x * 2 + c
    up, down = lax.rem(z + 1, NZ), lax.rem(z + NZ - 1, NZ)
    peers = []
    for j in range(NDP * NY):
        if j:
            p, q = lax.rem(n + j // NY, NDP), lax.rem(y + j, NY)
            peers.append({"y": q, "x": p // 2, "c": lax.rem(p, 2)})
    greet(peers + [{"z": up}, {"z": down}])

    def plan(j, i):
        p = lax.rem(n + j, NDP)
        head = n * 3 + i
        query = head < QUERY_HEADS
        slot = jnp.where(query, lax.rem(head, 4), head // 4)
        target = jnp.where(query, head // 4, lax.rem(head, 4))
        src = proj.at[p, :, i * HEAD : (i + 1) * HEAD]
        dst = heads.at[slot, y]
        there = lambda: send(
            src, dst, (hs.at[j, i], hr.at[slot, y]), y=target, x=p // 2, c=lax.rem(p, 2)
        )
        stay = lambda: pltpu.make_async_copy(src, dst, hr.at[slot, y])
        return there, stay, target == y

    for i in (2, 1, 0):
        for j in range(1, NDP):
            plan(j, i)[0]().start()
        there, stay, own = plan(0, i)

        @pl.when(own)
        def _():
            stay().start()

        @pl.when(jnp.logical_not(own))
        def _():
            there().start()

    def arrived(slot, k):
        pltpu.make_async_copy(heads.at[slot, k], heads.at[slot, k], hr.at[slot, k]).wait()

    ups, downs, keeps = [], [], []
    for t in range(1, 5):
        for i in range(2):
            if t == 1:
                for k in range(NY):
                    arrived(4 + i, k)
                keep = pltpu.make_async_copy(heads.at[4 + i], kv.at[i, z], local.at[i])
                keep.start()
                keeps.append(keep)
                above = below = heads.at[4 + i]
            else:
                ups[2 * (t - 2) + i].wait_recv()
                downs[2 * (t - 2) + i].wait_recv()
                above = kv.at[i, lax.rem(z + NZ - (t - 1), NZ)]
                below = kv.at[i, lax.rem(z + (t - 1), NZ)]
            copy = send(above, kv.at[i, lax.rem(z + NZ - (t - 1), NZ)], (rs.at[t - 1, i], rr.at[t - 1, i]), z=up)
            copy.start()
            ups.append(copy)
            if t < 4:
                copy = send(below, kv.at[i, lax.rem(z + (t - 1), NZ)], (ls.at[t - 1, i], lr.at[t - 1, i]), z=down)
                copy.start()
                downs.append(copy)
    for slot in range(4):
        for k in range(NY):
            arrived(slot, k)
    for i in range(2):
        ups[6 + i].wait_recv()
    for copy in ups + downs:
        copy.wait_send()
    for copy in keeps:
        copy.wait()
    for i in range(3):
        for j in range(1, NDP):
            plan(j, i)[0]().wait_send()
        there, stay, own = plan(0, i)

        @pl.when(jnp.logical_not(own))
        def _():
            there().wait_send()


def to_heads(proj):
    dma = pltpu.SemaphoreType.DMA
    return pl.pallas_call(
        heads_kernel,
        in_specs=[ANY],
        out_specs=[ANY, ANY],
        out_shape=[
            jax.ShapeDtypeStruct((6, NY, ROWS, HEAD), BF),
            jax.ShapeDtypeStruct((2, NZ, NY, ROWS, HEAD), BF),
        ],
        scratch_shapes=[
            dma((2,)),
            dma((NDP, 3)),
            dma((6, NY)),
            dma((4, 2)),
            dma((4, 2)),
            dma((3, 2)),
            dma((3, 2)),
        ],
        compiler_params=pltpu.CompilerParams(collective_id=1, has_side_effects=True),
        name="to_heads",
    )(proj)


CHUNK = 352
QM = 256
QO = 32
KM = NS * MAIN


def attention_kernel(
    heads_ref, kv_ref, gy_ref, gz_ref, spot_ref, owner_ref,
    om_ref, oo_ref, dq_ref, dkv_ref,
    k_ref, v_ref, kt, vt, g_ref, qo_ref, go_ref, scores, dk, dv, kidx_ref, line, qidx_ref, qoidx_ref,
):
    chunks = PATCHES // CHUNK
    z = lax.axis_index("z")
    spot = spot_ref[0, 0].astype(jnp.int32)

    for t in range(0, PATCHES, 128):
        w = min(128, PATCHES - t)
        r = lax.broadcasted_iota(jnp.int32, (w, w), 0)
        j = lax.broadcasted_iota(jnp.int32, (w, w), 1)
        own = owner_ref[0:1, t : t + w] == (r & 31)
        hit = jnp.where(own & ((r >> 5) == (j >> 5)), 1.0, 0.0).astype(BF)
        down = lax.broadcasted_iota(jnp.int32, (w, 128), 0).astype(F32).astype(BF)
        along = lax.broadcasted_iota(jnp.int32, (16, w), 1).astype(F32).astype(BF)
        scores[t : t + w, 0:128] = dot(hit, down) + float(t)
        line[:, t : t + w] = (
            lax.dot_general(along, hit, (((1,), (1,)), ((), ())), preferred_element_type=F32)
            + float(t)
        )[0:8]
    row = lax.broadcasted_iota(jnp.int32, (KM, 128), 0)
    kidx_ref[0:KM, :] = jnp.where(
        row < MAIN * (spot + 1), scores[0:KM, 0:128], scores[MAIN:PATCHES, 0:128]
    )
    base = MAIN * (spot + 1)
    row = lax.broadcasted_iota(jnp.int32, (MAIN, 128), 0)
    place = scores[pl.ds(pl.multiple_of(base, MAIN), MAIN), 0:128] - (
        base + 32 * (row >> 5)
    ).astype(F32)
    row = lax.broadcasted_iota(jnp.int32, (MAIN, MAIN), 0)
    col = lax.broadcasted_iota(jnp.int32, (MAIN, MAIN), 1)
    mix = jnp.where(col == (row & 1) * 32 + (row >> 1), 1.0, 0.0).astype(BF)
    place = dot(mix, place.astype(BF))
    row = lax.broadcasted_iota(jnp.int32, (MAIN, 128), 0)
    kidx_ref[KM:PATCHES, :] = place + (base + 32 * (row & 1)).astype(F32)
    window = line[0:1, pl.ds(pl.multiple_of(z * QM, QM), QM + 128)]
    col = lax.broadcasted_iota(jnp.int32, (1, QM), 1) + z * QM
    qidx_ref[...] = jnp.where(col < base, window[:, 0:QM], window[:, MAIN : MAIN + QM])
    row = lax.broadcasted_iota(jnp.int32, (MAIN, QO), 0)
    col = lax.broadcasted_iota(jnp.int32, (MAIN, QO), 1)
    mine = jnp.where(row == 8 * z + (col & 7), 1.0, 0.0).astype(BF)
    col = lax.broadcasted_iota(jnp.int32, (1, QO), 1)
    qoidx_ref[...] = dot_t(place.astype(BF), mine)[0:1] + (base + 32 * (col & 1)).astype(F32)

    for i, ref in enumerate((k_ref, v_ref)):
        for k in range(NZ):
            ref[k * QM : (k + 1) * QM, :] = kv_ref[i, k, :, 0:MAIN, :].reshape(QM, HEAD)
            for j in range(NY):
                at = KM + 2 * (k * NY + j)
                ref[at : at + 2, :] = kv_ref[i, k, j, MAIN : MAIN + 2, :]
    kt[...] = k_ref[...].astype(F32).T.astype(BF)
    vt[...] = v_ref[...].astype(F32).T.astype(BF)
    dk[...] = jnp.zeros_like(dk)
    dv[...] = jnp.zeros_like(dv)

    row = lax.broadcasted_iota(jnp.int32, (QM, 512), 0)
    col = lax.broadcasted_iota(jnp.int32, (QM, 512), 1)
    late = jnp.where(z * NY + (row >> 6) > spot, 2, 0)
    pick = jnp.where(col == (row & 31) * 16 + (row >> 5) + late, 1.0, 0.0).astype(BF)
    g_ref[...] = dot(pick, gz_ref[...].reshape(512, 512)).astype(BF)
    row = lax.broadcasted_iota(jnp.int32, (16, 66), 0)
    col = lax.broadcasted_iota(jnp.int32, (16, 66), 1)
    pick = jnp.where((col == 2 * spot + 2 + row) & (row < 2), 1.0, 0.0).astype(BF)
    for j in range(NY):
        extra = dot(pick, gy_ref[j]).astype(BF)
        for h in range(4):
            at = 8 * h + 2 * j
            go_ref[at : at + 2, :] = extra[0:2, HEAD * h : HEAD * (h + 1)]
            qo_ref[at : at + 2, :] = heads_ref[h, j, MAIN : MAIN + 2, :]

    def span(c):
        return pl.ds(pl.multiple_of(c * CHUNK, 32), CHUNK)

    def block(q, g, qidx, width):
        qt = q.astype(F32).T.astype(BF)
        gt32 = g.astype(F32).T
        gt = gt32.astype(BF)

        peak = jnp.full((1, width), -jnp.inf, F32)
        for c in range(chunks):
            at = span(c)
            s = dot(k_ref[at, :], qt) * FACTOR
            index = kidx_ref[at, :]
            index = jnp.concatenate([index, index], axis=1) if width > 128 else index[:, :width]
            s = jnp.where(index <= qidx, s, -jnp.inf)
            scores[at, :width] = s
            peak = jnp.maximum(peak, jnp.max(s, axis=0, keepdims=True))
        total = jnp.zeros((1, width), F32)
        for c in range(chunks):
            at = span(c)
            p = jnp.exp(scores[at, :width] - peak)
            scores[at, :width] = p
            total = total + jnp.sum(p, axis=0, keepdims=True)
        inverse = 1.0 / total
        out_t = jnp.zeros((HEAD, width), F32)
        for c in range(chunks):
            at = span(c)
            a = scores[at, :width] * inverse
            scores[at, :width] = a
            low = a.astype(BF)
            out_t = out_t + dot(vt[:, c * CHUNK : (c + 1) * CHUNK], low)
            dv[at, :] += dot(low, g)
        delta = jnp.sum(gt32 * out_t, axis=0, keepdims=True)
        dq_t = jnp.zeros((HEAD, width), F32)
        for c in range(chunks):
            at = span(c)
            da = dot(v_ref[at, :], gt)
            ds = (scores[at, :width] * (da - delta)).astype(BF)
            dq_t = dq_t + dot(kt[:, c * CHUNK : (c + 1) * CHUNK], ds)
            dk[at, :] += dot(ds, q)
        return out_t, (dq_t * FACTOR).T.astype(BF)

    row = lax.broadcasted_iota(jnp.int32, (QM, QM), 0)
    col = lax.broadcasted_iota(jnp.int32, (QM, QM), 1)
    turn = jnp.where(col == (row & 7) * 32 + (row >> 3), 1.0, 0.0).astype(BF)

    @pl.loop(0, 4)
    def _(h):
        q = heads_ref[h, :, 0:MAIN, :].reshape(QM, HEAD)
        out_t, dq = block(q, g_ref[:, lanes(h)], qidx_ref[...], QM)
        moved = lax.dot_general(
            turn, out_t.astype(BF), (((1,), (1,)), ((), ())), preferred_element_type=F32
        )
        om_ref[:, :, lanes(h)] = moved.astype(BF).reshape(NS, 8, HEAD)
        dq_ref[h, :, 0:MAIN, :] = dq.reshape(NY, MAIN, HEAD)

    out_t, dq = block(qo_ref[...], go_ref[...], qoidx_ref[...], QO)
    out = out_t.T.astype(BF)
    oo_ref[...] = jnp.zeros_like(oo_ref)
    dq_ref[:, :, MAIN:ROWS, :] = jnp.zeros((4, NY, ROWS - MAIN, HEAD), BF)
    for h in range(4):
        for j in range(NY):
            at = 8 * h + 2 * j
            oo_ref[j, 0:2, HEAD * h : HEAD * (h + 1)] = out[at : at + 2]
            dq_ref[h, j, MAIN : MAIN + 2, :] = dq[at : at + 2]
    for i, (ref, scale) in enumerate(((dk, FACTOR), (dv, 1.0))):
        for k in range(NZ):
            block_rows = (ref[k * QM : (k + 1) * QM, :] * scale).astype(BF)
            dkv_ref[i, k, :, 0:MAIN, :] = block_rows.reshape(NY, MAIN, HEAD)
        extra = (ref[KM:PATCHES, :] * scale).astype(BF)
        dkv_ref[i, :, :, MAIN:ROWS, :] = jnp.zeros((NZ, NY, ROWS - MAIN, HEAD), BF)
        for k in range(NZ):
            for j in range(NY):
                at = 2 * (k * NY + j)
                dkv_ref[i, k, j, MAIN : MAIN + 2, :] = extra[at : at + 2]


def attention(heads, kv, gy, gz, spot, owner):
    return pl.pallas_call(
        attention_kernel,
        in_specs=[VM] * 4 + [pl.BlockSpec(memory_space=pltpu.SMEM), VM],
        out_specs=[VM] * 4,
        out_shape=[
            jax.ShapeDtypeStruct((NS, 8, 512), BF),
            jax.ShapeDtypeStruct((NY, 8, 512), BF),
            jax.ShapeDtypeStruct((4, NY, ROWS, HEAD), BF),
            jax.ShapeDtypeStruct((2, NZ, NY, ROWS, HEAD), BF),
        ],
        scratch_shapes=[
            pltpu.VMEM((PATCHES, HEAD), BF),
            pltpu.VMEM((PATCHES, HEAD), BF),
            pltpu.VMEM((HEAD, PATCHES), BF),
            pltpu.VMEM((HEAD, PATCHES), BF),
            pltpu.VMEM((QM, 512), BF),
            pltpu.VMEM((QO, HEAD), BF),
            pltpu.VMEM((QO, HEAD), BF),
            pltpu.VMEM((PATCHES, QM), F32),
            pltpu.VMEM((PATCHES, HEAD), F32),
            pltpu.VMEM((PATCHES, HEAD), F32),
            pltpu.VMEM((PATCHES, 128), F32),
            pltpu.VMEM((8, 2304), F32),
            pltpu.VMEM((1, QM), F32),
            pltpu.VMEM((1, QO), F32),
        ],
        compiler_params=pltpu.CompilerParams(vmem_limit_bytes=VMEM_LIMIT),
        name="attention",
    )(heads, kv, gy, gz, spot, owner)


def columns_kernel(
    dq, dkv, cols, ubuf, usum, dbuf, dsum, red, hs, hr, rs, rr, ls, lr
):
    z, y, x, c = here()
    n = x * 2 + c
    up, down = lax.rem(z + 1, NZ), lax.rem(z + NZ - 1, NZ)
    peers = []
    for j in range(1, NDP * NY):
        p, q = lax.rem(n + j // NY, NDP), lax.rem(y + j, NY)
        peers.append({"y": q, "x": p // 2, "c": lax.rem(p, 2)})
    greet(peers + [{"z": up}, {"z": down}])

    def plan(slot, j):
        k = lax.rem(y + j, NY)
        head = y * 4 + slot if slot < 4 else slot * 4 + y
        d, i = head // 3, lax.rem(head, 3)
        src = dq.at[slot, k] if slot < 4 else red.at[slot - 4, k]
        dst = cols.at[n, :, lanes(i)]
        there = lambda: send(
            src, dst, (hs.at[slot, j], hr.at[n, i]), y=k, x=d // 2, c=lax.rem(d, 2)
        )
        stay = lambda: pltpu.make_async_copy(src, dst, hr.at[n, i])
        return there, stay, d == n

    def start(slot):
        for j in range(1, NY):
            plan(slot, j)[0]().start()
        there, stay, own = plan(slot, 0)

        @pl.when(own)
        def _():
            stay().start()

        @pl.when(jnp.logical_not(own))
        def _():
            there().start()

    def sent(slot):
        for j in range(1, NY):
            plan(slot, j)[0]().wait_send()
        there, _, own = plan(slot, 0)

        @pl.when(jnp.logical_not(own))
        def _():
            there().wait_send()

    def at(k):
        return lax.rem(z + k, NZ)

    ups, downs = {}, {}
    for t in range(1, 5):
        for i in range(2):
            if t == 1:
                above, below = dkv.at[i, at(4)], dkv.at[i, at(5)]
            else:
                ups[t - 1, i].wait_recv()
                usum[i, t - 2] = add(ubuf[i, t - 2], dkv[i, at(5 - t)])
                above = usum.at[i, t - 2]
                if t < 4:
                    downs[t - 1, i].wait_recv()
                    dsum[i, t - 2] = add(dbuf[i, t - 2], dkv[i, at(4 + t)])
                    below = dsum.at[i, t - 2]
            ups[t, i] = send(above, ubuf.at[i, t - 1], (rs.at[t - 1, i], rr.at[t - 1, i]), z=up)
            ups[t, i].start()
            if t < 4:
                downs[t, i] = send(
                    below, dbuf.at[i, t - 1], (ls.at[t - 1, i], lr.at[t - 1, i]), z=down
                )
                downs[t, i].start()
        if t == 1:
            for slot in range(4):
                start(slot)
    for i in range(2):
        downs[3, i].wait_recv()
        ups[4, i].wait_recv()
        red[i] = add(ubuf[i, 3], dbuf[i, 2], dkv[i, z])
        start(4 + i)
    for p in range(NDP):
        for i in range(3):
            block = cols.at[p, :, i * HEAD : (i + 1) * HEAD]
            pltpu.make_async_copy(block, block, hr.at[p, i]).wait()
    for copy in (*ups.values(), *downs.values()):
        copy.wait_send()
    for slot in range(6):
        sent(slot)


def to_columns(dq, dkv):
    dma = pltpu.SemaphoreType.DMA
    part = (NY, ROWS, HEAD)
    return pl.pallas_call(
        columns_kernel,
        in_specs=[VM, VM],
        out_specs=ANY,
        out_shape=jax.ShapeDtypeStruct((NDP, ROWS, COLS), BF),
        scratch_shapes=[
            pltpu.VMEM((2, 4, *part), BF),
            pltpu.VMEM((2, 3, *part), BF),
            pltpu.VMEM((2, 3, *part), BF),
            pltpu.VMEM((2, 2, *part), BF),
            pltpu.VMEM((2, *part), BF),
            dma((6, NY)),
            dma((NDP, 3)),
            dma((4, 2)),
            dma((4, 2)),
            dma((3, 2)),
            dma((3, 2)),
        ],
        compiler_params=pltpu.CompilerParams(
            collective_id=2, has_side_effects=True, vmem_limit_bytes=VMEM_LIMIT
        ),
        name="to_columns",
    )(dq, dkv)


def products_kernel(
    main_ref, over_ref, cols_ref, weight_ref,
    part_ref, back_ref, extra_ref,
    cm, co, cmt, cot, over_rows,
):
    @pl.when(pl.program_id(0) == 0)
    def _():
        for n in range(NDP):
            cm[MAIN * n : MAIN * (n + 1), :] = cols_ref[n, 0:MAIN, :]
            co[2 * n : 2 * n + 2, :] = cols_ref[n, MAIN : MAIN + 2, :]
        cmt[...] = cm[...].astype(F32).T.astype(BF)
        cot[...] = co[...].astype(F32).T.astype(BF)

    width = weight_ref.shape[0]
    for n in range(NDP):
        over_rows[2 * n : 2 * n + 2, :] = over_ref[n]
    part = dot(cmt[...], main_ref[...].reshape(NDP * MAIN, width)) + dot(cot[...], over_rows[...])
    part = part.astype(BF)
    for k in range(NY):
        part_ref[0, k] = part[:, HEAD * k : HEAD * (k + 1)]
    turn = (((1,), (1,)), ((), ()))
    back = lax.dot_general(cm[...], weight_ref[...], turn, preferred_element_type=F32)
    back_ref[...] = back.astype(BF).reshape(NDP, MAIN, width)
    extra = lax.dot_general(co[...], weight_ref[...], turn, preferred_element_type=F32)
    extra = extra.astype(BF)
    for n in range(NDP):
        extra_ref[n] = extra[2 * n : 2 * n + 2]


def products(all_main, all_over, cols, weight):
    steps = NZ
    width = DG // steps
    return pl.pallas_call(
        products_kernel,
        grid=(steps,),
        in_specs=[
            pl.BlockSpec((NDP, MAIN, width), lambda i: (0, 0, i)),
            pl.BlockSpec((NDP, 2, width), lambda i: (0, 0, i)),
            pl.BlockSpec((NDP, ROWS, COLS), lambda i: (0, 0, 0)),
            pl.BlockSpec((width, COLS), lambda i: (i, 0)),
        ],
        out_specs=[
            pl.BlockSpec((1, NY, COLS, HEAD), lambda i: (i, 0, 0, 0)),
            pl.BlockSpec((NDP, MAIN, width), lambda i: (0, 0, i)),
            pl.BlockSpec((NDP, 2, width), lambda i: (0, 0, i)),
        ],
        out_shape=[
            jax.ShapeDtypeStruct((NZ, NY, COLS, HEAD), BF),
            jax.ShapeDtypeStruct((NDP, MAIN, DG), BF),
            jax.ShapeDtypeStruct((NDP, 2, DG), BF),
        ],
        scratch_shapes=[
            pltpu.VMEM((NDP * MAIN, COLS), BF),
            pltpu.VMEM((16, COLS), BF),
            pltpu.VMEM((COLS, NDP * MAIN), BF),
            pltpu.VMEM((COLS, 16), BF),
            pltpu.VMEM((16, width), BF),
        ],
        compiler_params=pltpu.CompilerParams(vmem_limit_bytes=VMEM_LIMIT),
        name="products",
    )(all_main, all_over, cols, weight)


LONG = 256
SHORT = COLS - LONG


def sums_kernel(
    back, extra, w, om, oo,
    pooled, over_all, wgrad, am, ao,
    own, sib, chip, xa, xb, xr, xl, sxa, sxb,
    ya, yb, yr, yl, sa, sb, wy, wz, ubuf, usum, dbuf, dsum, wb, wq, obuf, omz, ov, oz,
    local, cs, cr, xs, xrv, ws, wr, us, ur, ds, dr, zs, zr, os_, or_, ps, pr,
):
    z, y, x, c = here()
    n = x * 2 + c
    right, left, far = lax.rem(x + 1, NX), lax.rem(x + 3, NX), lax.rem(x + 2, NX)
    yn, yp, yf = lax.rem(y + 1, NY), lax.rem(y + 3, NY), lax.rem(y + 2, NY)
    up, down = lax.rem(z + 1, NZ), lax.rem(z + NZ - 1, NZ)
    ys_at = [lax.rem(y + j, NY) for j in range(NY)]
    zs_at = [lax.rem(z + j, NZ) for j in range(NZ)]
    dp_at = [lax.rem(n + j, NDP) for j in range(NDP)]
    greet(
        [{"y": ys_at[j]} for j in range(1, NY)]
        + [{"z": zs_at[j]} for j in range(1, NZ)]
        + [{"x": p // 2, "c": lax.rem(p, 2)} for p in dp_at[1:]]
    )
    copies, stays = [], []

    def go(src, dst, pair, **device):
        copy = send(src, dst, pair, **device)
        copy.start()
        copies.append(copy)
        return copy

    def stay(src, dst):
        copy = pltpu.make_async_copy(src, dst, local.at[len(stays)])
        copy.start()
        stays.append(copy)
        return copy

    waited = []

    def done(copy):
        copy.wait()
        waited.append(copy)

    def at(k):
        return lax.rem(z + k, NZ)

    order = (far, right, left, x)
    halves = [
        go(back.at[p * 2 + 1 - c], sib.at[p], (cs.at[k], cr.at[k]), c=1 - c)
        for k, p in enumerate(order)
    ]
    loads = [stay(back.at[p * 2 + c], own.at[p]) for p in order]

    overs = [
        go(extra.at[p], obuf.at[n], (ps.at[j], pr.at[j]), x=p // 2, c=lax.rem(p, 2))
        for j, p in enumerate(dp_at)
        if j
    ]
    here_o = stay(extra.at[n], obuf.at[n])

    short, long = pl.ds(LONG, SHORT), pl.ds(0, LONG)
    ups, downs = {}, {}

    def ring(t):
        for i in range(2):
            some = pl.ds(2 * i, 2)
            if t == 1:
                above, below = w.at[at(4), some, short], w.at[at(5), some, short]
            else:
                ups[t - 1, i].wait_recv()
                usum[t - 2, i] = add(ubuf[t - 2, i], w[at(5 - t), some, short])
                above = usum.at[t - 2, i]
                if t < 4:
                    downs[t - 1, i].wait_recv()
                    dsum[t - 2, i] = add(dbuf[t - 2, i], w[at(4 + t), some, short])
                    below = dsum.at[t - 2, i]
            ups[t, i] = go(above, ubuf.at[t - 1, i], (us.at[t - 1, i], ur.at[t - 1, i]), z=up)
            if t < 4:
                downs[t, i] = go(
                    below, dbuf.at[t - 1, i], (ds.at[t - 1, i], dr.at[t - 1, i]), z=down
                )

    ring(1)
    lo, hi = pl.ds(0, 4), pl.ds(4, 4)
    w_a = go(w.at[lo, yf, long], ya, (ws.at[0], wr.at[0]), y=yn)
    w_b = go(w.at[hi, yf, long], yb, (ws.at[1], wr.at[1]), y=yp)
    w_hi = go(w.at[hi, yn, long], yr.at[hi], (ws.at[2], wr.at[2]), y=yn)
    w_lo = go(w.at[lo, yp, long], yl.at[lo], (ws.at[3], wr.at[3]), y=yp)

    first, second = pl.ds(0, DG // 2), pl.ds(DG // 2, DG // 2)
    for k, p in enumerate(order):
        done(loads[k])
        halves[k].wait_recv()
        chip[p] = add(own[p], sib[p])
        if k == 0:
            x_a = go(chip.at[p, :, first], xa, (xs.at[0], xrv.at[0]), x=right)
            x_b = go(chip.at[p, :, second], xb, (xs.at[1], xrv.at[1]), x=left)
        if k == 1:
            x_hi = go(chip.at[p, :, second], xr.at[:, second], (xs.at[2], xrv.at[2]), x=right)
        if k == 2:
            x_lo = go(chip.at[p, :, first], xl.at[:, first], (xs.at[3], xrv.at[3]), x=left)

    for copy in overs:
        copy.wait_recv()
    done(here_o)
    ov[...] = add(*[obuf[k] for k in range(NDP)])
    over_z = [go(ov, oz.at[z], (zs.at[1, j], zr.at[1, j]), z=zs_at[j]) for j in range(1, NZ)]
    keep_oz = stay(ov, oz.at[z])
    ring(2)
    w_a.wait_recv()
    sa[...] = add(ya[...], w[lo, yn, long])
    w_lo2 = go(sa, yr.at[lo], (ws.at[4], wr.at[4]), y=yn)
    w_b.wait_recv()
    sb[...] = add(yb[...], w[hi, yp, long])
    w_hi2 = go(sb, yl.at[hi], (ws.at[5], wr.at[5]), y=yp)
    ring(3)
    x_a.wait_recv()
    sxa[...] = add(xa[...], chip[right, :, first])
    x_lo2 = go(sxa, xr.at[:, first], (xs.at[4], xrv.at[4]), x=right)
    x_b.wait_recv()
    sxb[...] = add(xb[...], chip[left, :, second])
    x_hi2 = go(sxb, xl.at[:, second], (xs.at[5], xrv.at[5]), x=left)
    for copy in over_z:
        copy.wait_recv()
    done(keep_oz)
    over_y = [
        go(oz, over_all.at[y], (os_.at[2, j], or_.at[2, j]), y=ys_at[j]) for j in range(1, NY)
    ]
    stay(oz, over_all.at[y])
    ring(4)
    rows_z = [
        go(om.at[zs_at[j]], omz.at[z], (zs.at[0, j], zr.at[0, j]), z=zs_at[j])
        for j in range(1, NZ)
    ]
    here_z = stay(om.at[z], omz.at[z])

    for copy in (w_hi, w_lo, w_lo2, w_hi2):
        copy.wait_recv()
    wy[...] = add(w[:, y, long], yr[...], yl[...])
    longs = [
        go(wy.at[zs_at[j]], wz.at[j], (zs.at[2, j], zr.at[2, j]), z=zs_at[j])
        for j in range(1, NZ)
    ]
    for i in range(2):
        downs[3, i].wait_recv()
        ups[4, i].wait_recv()
        some = pl.ds(2 * i, 2)
        wb[some] = add(w[z, some, short], ubuf[3, i], dbuf[2, i])
    shorts = [
        go(wb.at[ys_at[j]], wq.at[j], (os_.at[3, j], or_.at[3, j]), y=ys_at[j])
        for j in range(1, NY)
    ]

    for copy in rows_z:
        copy.wait_recv()
    done(here_z)
    rows_y = []
    for j in range(1, NY):
        k = ys_at[j]
        rows_y.append(go(omz.at[:, k], am.at[y], (os_.at[0, j], or_.at[0, j]), y=k))
        rows_y.append(go(oo.at[k], ao.at[y], (os_.at[1, j], or_.at[1, j]), y=k))
    stay(omz.at[:, y], am.at[y])
    stay(oo.at[y], ao.at[y])

    for copy in (x_hi, x_lo, x_lo2, x_hi2):
        copy.wait_recv()
    pooled[...] = add(chip[x], xr[...], xl[...])
    for copy in shorts:
        copy.wait_recv()
    total = wb[y].astype(F32)
    for j in range(1, NY):
        total = total + wq[j].astype(F32)
    wgrad[short, :] = total
    for copy in longs:
        copy.wait_recv()
    total = wy[z].astype(F32)
    for j in range(1, NZ):
        total = total + wz[j].astype(F32)
    wgrad[long, :] = total
    for copy in (*over_y, *rows_y):
        copy.wait_recv()
    for copy in copies:
        copy.wait_send()
    for copy in stays:
        if not any(copy is other for other in waited):
            copy.wait()


def sums(back, extra, part, om, oo):
    dma = pltpu.SemaphoreType.DMA
    rows = (MAIN, DG)
    half = (MAIN, DG // 2)
    long = (LONG, HEAD)
    short = (2, SHORT, HEAD)
    return pl.pallas_call(
        sums_kernel,
        in_specs=[ANY, ANY, VM, ANY, ANY],
        out_specs=[VM, ANY, VM, ANY, ANY],
        out_shape=[
            jax.ShapeDtypeStruct(rows, BF),
            jax.ShapeDtypeStruct((NY, NZ, 2, DG), BF),
            jax.ShapeDtypeStruct((COLS, HEAD), F32),
            jax.ShapeDtypeStruct((NY, NZ, 8, 512), BF),
            jax.ShapeDtypeStruct((NY, 8, 512), BF),
        ],
        scratch_shapes=[
            *[pltpu.VMEM((NX, *rows), BF)] * 3,
            *[pltpu.VMEM(half, BF)] * 2,
            *[pltpu.VMEM(rows, BF)] * 2,
            *[pltpu.VMEM(half, BF)] * 2,
            *[pltpu.VMEM((4, *long), BF)] * 2,
            *[pltpu.VMEM((8, *long), BF)] * 2,
            *[pltpu.VMEM((4, *long), BF)] * 2,
            *[pltpu.VMEM((8, *long), BF)] * 2,
            pltpu.VMEM((4, 2, *short), BF),
            pltpu.VMEM((3, 2, *short), BF),
            pltpu.VMEM((3, 2, *short), BF),
            pltpu.VMEM((2, 2, *short), BF),
            pltpu.VMEM((4, SHORT, HEAD), BF),
            pltpu.VMEM((4, SHORT, HEAD), BF),
            pltpu.VMEM((NDP, 2, DG), BF),
            pltpu.VMEM((NZ, NY, 8, 512), BF),
            pltpu.VMEM((2, DG), BF),
            pltpu.VMEM((NZ, 2, DG), BF),
            dma((10,)),
            dma((4,)),
            dma((4,)),
            dma((6,)),
            dma((6,)),
            dma((6,)),
            dma((6,)),
            dma((4, 2)),
            dma((4, 2)),
            dma((3, 2)),
            dma((3, 2)),
            dma((3, NZ)),
            dma((3, NZ)),
            dma((4, NY)),
            dma((4, NY)),
            dma((NDP,)),
            dma((NDP,)),
        ],
        compiler_params=pltpu.CompilerParams(
            collective_id=3, has_side_effects=True, vmem_limit_bytes=VMEM_LIMIT
        ),
        name="sums",
    )(back, extra, part, om, oo)


def body(byte_states, byte_patch, patch_owner, qkv_weight, attention_output_gradient):
    main, over, slot, flag, band = pool(
        byte_patch, patch_owner, byte_states, attention_output_gradient
    )
    all_main, all_over, spot, gy, gz = gather_rows(
        main, over, flag, band, attention_output_gradient
    )
    heads, kv = to_heads(project(all_main, all_over, qkv_weight))
    om, oo, dq, dkv = attention(heads, kv, gy, gz, spot, patch_owner)
    cols = to_columns(dq, dkv)
    part, back, extra = products(all_main, all_over, cols, qkv_weight)
    om = om.reshape(NZ, NY, 8, 512)
    pooled, over_back, wide, am, ao = sums(back, extra, part, om, oo)
    state_grad, att, weight_grad = spread(slot, pooled, over_back, am, ao, spot, wide)
    return att, state_grad, weight_grad


def solution(mesh):
    finer = Mesh(mesh.devices.reshape(NZ, NY, NX, NC), ("z", "y", "x", "c"))
    placed = (P(DP, SEQ, None), P(DP, SEQ), P(DP, None), P(None, DP), P(DP, SEQ, None))
    return jax.shard_map(
        body,
        mesh=finer,
        in_specs=placed,
        out_specs=(P(DP, SEQ, None), P(DP, SEQ, None), P(SEQ, DP)),
        check_vma=False,
    )
```

```python
import functools

import jax
import jax.numpy as jnp
from jax import lax
from jax.experimental import pallas as pl
from jax.experimental.pallas import tpu as pltpu
from jax.sharding import Mesh
from jax.sharding import PartitionSpec as P

QUERY_HEADS = 16
KEY_VALUE_HEADS = 4
HEAD = 128
FACTOR = HEAD ** (-0.5)
NZ, NY, NX, NC = 8, 4, 4, 2
NS, NDP = NZ * NY, NX * NC
SEQ = ("z", "y")
DP = ("x", "c")
MAIN = 64
BYTES = 256
DG = 4096
PATCHES = 2112
COLS = 384
BF = jnp.bfloat16
F32 = jnp.float32
VMEM_LIMIT = 56 << 20


def dot(a, b):
    return jnp.dot(a, b, preferred_element_type=F32)


def dot_t(a, b):
    return lax.dot_general(a, b, (((0,), (0,)), ((), ())), preferred_element_type=F32)


def pool_kernel(
    ids_ref, owner_ref, states_ref, grad_ref,
    main_ref, over_ref, slot_ref, flag_ref, band_ref,
    onehot_ref,
):
    s = lax.axis_index("z") * NY + lax.axis_index("y")

    @pl.when(pl.program_id(0) == 0)
    def _():
        ids = ids_ref[...]
        first = jnp.min(ids, axis=1, keepdims=True)
        last = jnp.max(ids, axis=1, keepdims=True)
        group = (ids - first) >> 5
        patch = lax.broadcasted_iota(jnp.int32, (PATCHES, BYTES), 0)
        hit = jnp.where(patch == ids, 1.0, 0.0).astype(BF)
        owner = jnp.broadcast_to(owner_ref[...].astype(F32), (16, PATCHES)).astype(BF)
        byte_owner = dot(owner, hit)[0:1].astype(jnp.int32)
        over = MAIN + (byte_owner & 3) * 16 + (byte_owner >> 2) * 2 + (group - 2)
        slot = jnp.where(group < 2, group * 32 + byte_owner, over)
        slot_ref[...] = slot
        rows = lax.broadcasted_iota(jnp.int32, (2 * MAIN, BYTES), 0)
        onehot_ref[...] = jnp.where(rows == slot, 1.0, 0.0)
        spike = jnp.where(last - first >= MAIN, s.astype(F32), 0.0)
        flag_ref[...] = jnp.broadcast_to(spike, (8, 128))

    onehot = onehot_ref[...]
    counts = jnp.maximum(jnp.sum(onehot, axis=1, keepdims=True), 1.0)
    pooled = (dot(onehot.astype(BF), states_ref[0]) / counts).astype(BF)
    main_ref[...] = pooled[:MAIN]
    over_ref[...] = pooled[MAIN:].reshape(NY, 16, pooled.shape[1])
    grad = grad_ref[0]
    for z in range(NZ - 1):
        band_ref[z] = grad[8 * z : 8 * z + 16]
    band_ref[NZ - 1] = jnp.zeros_like(band_ref[NZ - 1])
    band_ref[NZ - 1, 0:10, :] = grad[56:66]


def pool(byte_patch, patch_owner, byte_states, grad):
    steps = 4
    width = DG // steps
    return pl.pallas_call(
        pool_kernel,
        grid=(steps,),
        in_specs=[
            pl.BlockSpec((1, BYTES), lambda i: (0, 0)),
            pl.BlockSpec((1, PATCHES), lambda i: (0, 0)),
            pl.BlockSpec((1, BYTES, width), lambda i: (0, 0, i)),
            pl.BlockSpec((1, 66, 512), lambda i: (0, 0, i)),
        ],
        out_specs=[
            pl.BlockSpec((MAIN, width), lambda i: (0, i)),
            pl.BlockSpec((NY, 16, width), lambda i: (0, 0, i)),
            pl.BlockSpec((1, BYTES), lambda i: (0, 0)),
            pl.BlockSpec((8, 128), lambda i: (0, 0)),
            pl.BlockSpec((NZ, 16, 512), lambda i: (0, 0, i)),
        ],
        out_shape=[
            jax.ShapeDtypeStruct((MAIN, DG), BF),
            jax.ShapeDtypeStruct((NY, 16, DG), BF),
            jax.ShapeDtypeStruct((1, BYTES), jnp.int32),
            jax.ShapeDtypeStruct((8, 128), F32),
            jax.ShapeDtypeStruct((NZ, 16, 2048), BF),
        ],
        scratch_shapes=[pltpu.VMEM((2 * MAIN, BYTES), F32)],
        name="pool",
    )(byte_patch, patch_owner, byte_states, grad)


MESH = pl.DeviceIdType.MESH
ANY = pl.BlockSpec(memory_space=pl.ANY)
VM = pl.BlockSpec(memory_space=pltpu.VMEM)


def add(*parts):
    if len(parts) == 2:
        return parts[0] + parts[1]
    total = parts[0].astype(F32)
    for part in parts[1:]:
        total = total + part.astype(F32)
    return total.astype(BF)


def here():
    return [lax.axis_index(name) for name in ("z", "y", "x", "c")]


def send(src, dst, pair, **device):
    return pltpu.make_async_remote_copy(
        src_ref=src, dst_ref=dst, send_sem=pair[0], recv_sem=pair[1],
        device_id=device, device_id_type=MESH,
    )


def greet(devices):
    barrier = pltpu.get_barrier_semaphore()
    for device in devices:
        pl.semaphore_signal(barrier, inc=1, device_id=device, device_id_type=MESH)
    pl.semaphore_wait(barrier, len(devices))


def spread_kernel(
    slot_ref, pooled_ref, over_ref, am_ref, ao_ref, spot_ref, wide_ref,
    out_ref, att_ref, weight_ref,
    rows_ref,
):
    @pl.when(pl.program_id(0) == 0)
    def _():
        weight_ref[...] = wide_ref[...].T

    slot = slot_ref[...]
    rows = lax.broadcasted_iota(jnp.int32, (2 * MAIN, BYTES), 0)
    onehot = jnp.where(rows == slot, 1.0, 0.0)
    counts = jnp.broadcast_to(jnp.sum(onehot, axis=1, keepdims=True), (2 * MAIN, 128))
    low = onehot.astype(BF)
    byte_count = jnp.maximum(dot_t(low, counts.astype(BF))[:, 0:1], 1.0)
    rows_ref[0:MAIN, :] = pooled_ref[0:MAIN, :]
    for j in range(NY):
        for k in range(NZ):
            at = MAIN + j * 16 + k * 2
            rows_ref[at : at + 2, :] = over_ref[j, k]
    out_ref[0] = (dot_t(low, rows_ref[...]) / byte_count).astype(BF)

    edge = 2 * spot_ref[0:1, 0:1].astype(jnp.int32) + 2
    row = lax.broadcasted_iota(jnp.int32, (66, 64), 0)
    col = lax.broadcasted_iota(jnp.int32, (66, 64), 1)
    keep = ((row < edge) & (col == row)) | ((row > edge + 1) & (col == row - 2))
    att = dot(jnp.where(keep, 1.0, 0.0).astype(BF), am_ref[0].reshape(64, 512))
    row = lax.broadcasted_iota(jnp.int32, (66, 16), 0)
    col = lax.broadcasted_iota(jnp.int32, (66, 16), 1)
    keep = (col == row - edge) & (col < 2)
    extra = jnp.concatenate([ao_ref[0], jnp.zeros((8, 512), BF)], axis=0)
    att = att + dot(jnp.where(keep, 1.0, 0.0).astype(BF), extra)
    att_ref[0] = att.astype(BF)


def spread(slot, pooled, over, am, ao, spot, wide):
    steps = 4
    width = DG // steps
    return pl.pallas_call(
        spread_kernel,
        grid=(steps,),
        in_specs=[
            pl.BlockSpec((1, BYTES), lambda i: (0, 0)),
            pl.BlockSpec((MAIN, width), lambda i: (0, i)),
            pl.BlockSpec((NY, NZ, 2, width), lambda i: (0, 0, 0, i)),
            pl.BlockSpec((1, NZ, 8, 512), lambda i: (i, 0, 0, 0)),
            pl.BlockSpec((1, 8, 512), lambda i: (i, 0, 0)),
            pl.BlockSpec((8, 128), lambda i: (0, 0)),
            pl.BlockSpec((COLS, HEAD), lambda i: (0, 0)),
        ],
        out_specs=[
            pl.BlockSpec((1, BYTES, width), lambda i: (0, 0, i)),
            pl.BlockSpec((1, 66, 512), lambda i: (0, 0, i)),
            pl.BlockSpec((HEAD, COLS), lambda i: (0, 0)),
        ],
        out_shape=[
            jax.ShapeDtypeStruct((1, BYTES, DG), BF),
            jax.ShapeDtypeStruct((1, 66, 2048), BF),
            jax.ShapeDtypeStruct((HEAD, COLS), F32),
        ],
        scratch_shapes=[pltpu.VMEM((2 * MAIN, width), BF)],
        name="spread",
    )(slot, pooled, over, am, ao, spot, wide)


ROWS = 72


def lanes(i):
    return pl.ds(pl.multiple_of(i * HEAD, HEAD), HEAD)


def front_kernel(
    main, over, flag, band, grad, weight,
    all_main, all_over, spot, gy, gz, heads, kv,
    rows, wide, extras, extra_rows, proj, ybuf, zsrc, zbuf, mine, fy, fsum, fz, gband,
    local, main_s, main_r, ys, yr, zs, zr, os_, or_, hs, hr, rs, rr, ls, lr,
):
    z, y, x, c = here()
    n = x * 2 + c
    ys_at = [lax.rem(y + j, NY) for j in range(NY)]
    zs_at = [lax.rem(z + j, NZ) for j in range(NZ)]
    xs_at = [lax.rem(x + j, NX) for j in range(NX)]
    right, left, twin = xs_at[1], xs_at[3], 1 - c
    up, down = zs_at[1], zs_at[7]
    deals = [(d, e) for d in range(NX) for e in range(2)]
    core = [c, twin]
    greet(
        [
            {"y": ys_at[j], "x": xs_at[d], "c": core[e]}
            for d, e in deals
            for j in range(NY)
            if d or e or j
        ]
        + [{"z": zs_at[j]} for j in range(1, NZ)]
    )
    copies, stays, waited = [], [], []

    def go(src, dst, pair, **device):
        copy = send(src, dst, pair, **device)
        copy.start()
        copies.append(copy)
        return copy

    def stay(src, dst):
        copy = pltpu.make_async_copy(src, dst, local.at[len(stays)])
        copy.start()
        stays.append(copy)
        return copy

    def done(copy):
        copy.wait()
        waited.append(copy)

    def half(block, i):
        return block.at[pl.ds(32 * i, 32), :]

    def pair(i):
        return main_s.at[i], main_r.at[i]

    def columns(h):
        return pl.ds(pl.multiple_of(h * 512, 512), 512)

    stage_y = []
    for j in range(1, NY):
        k = ys_at[j]
        stage_y.append(go(over.at[k], ybuf.at[y], (ys.at[0, j], yr.at[0, j]), y=k))
        stage_y.append(go(flag, fy.at[y], (ys.at[1, j], yr.at[1, j]), y=k))
    here_y = [stay(over.at[y], ybuf.at[y]), stay(flag, fy.at[y])]

    block = rows.at[n]
    right_a = go(half(main, 0), half(block, 0), pair(1), x=right)
    left_b = go(half(main, 1), half(block, 1), pair(2), x=left)
    right_b = go(half(main, 1), half(block, 1), pair(3), x=right)
    left_a = go(half(main, 0), half(block, 0), pair(4), x=left)
    to_twin = go(main, block, pair(0), c=twin)
    stay(main, all_main.at[n])
    here_w = stay(weight, wide)

    bands_z = [
        go(band.at[zs_at[j]], gband.at[z], (zs.at[2, j], zr.at[2, j]), z=zs_at[j])
        for j in range(1, NZ)
    ]
    here_band = stay(band.at[z], gband.at[z])

    for copy in stage_y:
        copy.wait_recv()
    for copy in here_y:
        done(copy)
    summed = add(ybuf[0], ybuf[1], ybuf[2], ybuf[3])
    for k in range(NZ):
        zsrc[k] = summed[2 * k : 2 * k + 2]
    fsum[...] = fy[0] + fy[1] + fy[2] + fy[3]
    stage_z = []
    for j in range(1, NZ):
        k = zs_at[j]
        stage_z.append(go(zsrc.at[k], zbuf.at[z], (zs.at[0, j], zr.at[0, j]), z=k))
        stage_z.append(go(fsum, fz.at[z], (zs.at[1, j], zr.at[1, j]), z=k))
    here_z = [stay(zsrc.at[z], zbuf.at[z]), stay(fsum, fz.at[z])]
    grads_y = [
        go(grad.at[0, :, columns(ys_at[j])], gy.at[y], (ys.at[2, j], yr.at[2, j]), y=ys_at[j])
        for j in range(1, NY)
    ]
    stay(grad.at[0, :, columns(y)], gy.at[y])

    def seq(d, e):
        return xs_at[d] * 2 + core[e]

    def project(blocks, tail=None):
        parts = [value for _, value in blocks] + ([] if tail is None else [tail])
        product = dot(jnp.concatenate(parts, axis=0), wide[...]).astype(BF)
        for k, (place, _) in enumerate(blocks):
            proj[place, 0:MAIN, :] = product[MAIN * k : MAIN * (k + 1)]
        return product[MAIN * len(blocks) :]

    done(here_w)
    to_twin.wait_recv()
    project([(n, main[...]), (seq(0, 1), rows[seq(0, 1)])])
    proj[:, MAIN:ROWS, :] = jnp.zeros((NDP, ROWS - MAIN, COLS), BF)

    for copy in stage_z:
        copy.wait_recv()
    for copy in here_z:
        done(copy)
    total = zbuf[0].astype(F32)
    found = fz[0]
    for k in range(1, NZ):
        total = total + zbuf[k].astype(F32)
        found = found + fz[k]
    mine[...] = total.astype(BF)
    spot[...] = found
    overs = [
        go(mine, extras.at[n], (os_.at[2 * d + e], or_.at[2 * d + e]), x=xs_at[d], c=core[e])
        for d, e in deals
        if d or e
    ]
    here_o = stay(mine, extras.at[n])

    from_left, from_right = rows.at[left * 2 + c], rows.at[right * 2 + c]
    far = rows.at[xs_at[2] * 2 + c]
    right_a.wait_recv()
    on_right = go(half(from_left, 0), half(from_left, 0), pair(5), x=right)
    left_b.wait_recv()
    on_left = go(half(from_right, 1), half(from_right, 1), pair(6), x=left)
    right_b.wait_recv()
    side_left = go(from_left, from_left, pair(7), c=twin)
    left_a.wait_recv()
    side_right = go(from_right, from_right, pair(8), c=twin)

    for copy in bands_z:
        copy.wait_recv()
    done(here_band)
    bands_y = [
        go(gband.at[:, :, columns(ys_at[j])], gz.at[:, y], (ys.at[3, j], yr.at[3, j]), y=ys_at[j])
        for j in range(1, NY)
    ]
    stay(gband.at[:, :, columns(y)], gz.at[:, y])

    for copy in overs:
        copy.wait_recv()
    done(here_o)
    for p in range(NDP):
        extra_rows[2 * p : 2 * p + 2, :] = extras[p]
    stay(extras, all_over)
    side_left.wait_recv()
    side_right.wait_recv()
    near = [seq(1, 0), seq(3, 0), seq(1, 1), seq(3, 1)]
    tail = project([(p, rows[p]) for p in near], extra_rows[...])
    for p in range(NDP):
        proj[p, MAIN : MAIN + 2, :] = tail[2 * p : 2 * p + 2]

    def plan(d, e, i):
        head = n * 3 + i
        query = head < QUERY_HEADS
        slot = jnp.where(query, lax.rem(head, 4), head // 4)
        target = jnp.where(query, head // 4, lax.rem(head, 4))
        src = proj.at[seq(d, e), :, i * HEAD : (i + 1) * HEAD]
        dst = heads.at[slot, y]
        there = lambda: send(
            src, dst, (hs.at[2 * d + e, i], hr.at[slot, y]), y=target, x=xs_at[d], c=core[e]
        )
        here_ = lambda: pltpu.make_async_copy(src, dst, hr.at[slot, y])
        return there, here_, target == y

    def scatter(d, e):
        for i in (2, 1, 0):
            there, here_, own = plan(d, e, i)
            if d or e:
                there().start()
            else:

                @pl.when(own)
                def _():
                    here_().start()

                @pl.when(jnp.logical_not(own))
                def _():
                    there().start()

    for d in (1, 3, 0):
        for e in range(2):
            scatter(d, e)
    on_right.wait_recv()
    side_a = go(half(far, 0), half(far, 0), pair(9), c=twin)
    on_left.wait_recv()
    side_b = go(half(far, 1), half(far, 1), pair(10), c=twin)
    side_a.wait_recv()
    side_b.wait_recv()
    project([(seq(2, e), rows[seq(2, e)]) for e in range(2)])
    for e in range(2):
        scatter(2, e)
    for d, e in deals:
        if d or e:
            stay(rows.at[seq(d, e)], all_main.at[seq(d, e)])

    def arrived(slot, k):
        pltpu.make_async_copy(heads.at[slot, k], heads.at[slot, k], hr.at[slot, k]).wait()

    ups, downs = {}, {}
    for t in range(1, 5):
        for i in range(2):
            above_at, below_at = lax.rem(z + NZ - (t - 1), NZ), lax.rem(z + (t - 1), NZ)
            if t == 1:
                for k in range(NY):
                    arrived(4 + i, k)
                stay(heads.at[4 + i], kv.at[i, z])
                above = below = heads.at[4 + i]
            else:
                ups[t - 1, i].wait_recv()
                downs[t - 1, i].wait_recv()
                above, below = kv.at[i, above_at], kv.at[i, below_at]
            if t < 4 or i == 0:
                ups[t, i] = go(
                    above, kv.at[i, above_at], (rs.at[t - 1, i], rr.at[t - 1, i]), z=up
                )
            if t < 4 or i == 1:
                downs[t, i] = go(
                    below, kv.at[i, below_at], (ls.at[t - 1, i], lr.at[t - 1, i]), z=down
                )
    for slot in range(4):
        for k in range(NY):
            arrived(slot, k)
    for copy in (ups[4, 0], downs[4, 1], *grads_y, *bands_y):
        copy.wait_recv()
    for copy in copies:
        copy.wait_send()
    for copy in stays:
        if not any(copy is other for other in waited):
            copy.wait()
    for d, e in deals:
        for i in range(3):
            there, _, own = plan(d, e, i)
            if d or e:
                there().wait_send()
            else:

                @pl.when(jnp.logical_not(own))
                def _():
                    there().wait_send()


def front(main, over, flag, band, grad, weight):
    dma = pltpu.SemaphoreType.DMA
    return pl.pallas_call(
        front_kernel,
        in_specs=[VM] * 5 + [ANY],
        out_specs=[ANY, ANY, VM, VM, ANY, VM, ANY],
        out_shape=[
            jax.ShapeDtypeStruct((NDP, MAIN, DG), BF),
            jax.ShapeDtypeStruct((NDP, 2, DG), BF),
            jax.ShapeDtypeStruct((8, 128), F32),
            jax.ShapeDtypeStruct((NY, 66, 512), BF),
            jax.ShapeDtypeStruct((NZ, NY, 16, 512), BF),
            jax.ShapeDtypeStruct((6, NY, ROWS, HEAD), BF),
            jax.ShapeDtypeStruct((2, NZ, NY, ROWS, HEAD), BF),
        ],
        scratch_shapes=[
            pltpu.VMEM((NDP, MAIN, DG), BF),
            pltpu.VMEM((DG, COLS), BF),
            pltpu.VMEM((NDP, 2, DG), BF),
            pltpu.VMEM((16, DG), BF),
            pltpu.VMEM((NDP, ROWS, COLS), BF),
            pltpu.VMEM((NY, 16, DG), BF),
            pltpu.VMEM((NZ, 2, DG), BF),
            pltpu.VMEM((NZ, 2, DG), BF),
            pltpu.VMEM((2, DG), BF),
            pltpu.VMEM((NY, 8, 128), F32),
            pltpu.VMEM((8, 128), F32),
            pltpu.VMEM((NZ, 8, 128), F32),
            pltpu.VMEM((NZ, 16, 2048), BF),
            dma((20,)),
            dma((11,)),
            dma((11,)),
            dma((4, NY)),
            dma((4, NY)),
            dma((3, NZ)),
            dma((3, NZ)),
            dma((NDP,)),
            dma((NDP,)),
            dma((NDP, 3)),
            dma((6, NY)),
            dma((4, 2)),
            dma((4, 2)),
            dma((4, 2)),
            dma((4, 2)),
        ],
        compiler_params=pltpu.CompilerParams(
            collective_id=0, has_side_effects=True, vmem_limit_bytes=VMEM_LIMIT
        ),
        name="front",
    )(main, over, flag, band, grad, weight)


CHUNK = 352
QM = 256
QO = 32
KM = NS * MAIN


def attention_kernel(
    heads_ref, kv_ref, gy_ref, gz_ref, spot_ref, owner_ref,
    om_ref, oo_ref, dq_ref, dkv_ref,
    k_ref, v_ref, kt, vt, g_ref, qo_ref, go_ref, scores, dk, dv, kidx_ref, line, qidx_ref, qoidx_ref,
):
    chunks = PATCHES // CHUNK
    z = lax.axis_index("z")
    spot = spot_ref[0, 0].astype(jnp.int32)

    for t in range(0, PATCHES, 128):
        w = min(128, PATCHES - t)
        r = lax.broadcasted_iota(jnp.int32, (w, w), 0)
        j = lax.broadcasted_iota(jnp.int32, (w, w), 1)
        own = owner_ref[0:1, t : t + w] == (r & 31)
        hit = jnp.where(own & ((r >> 5) == (j >> 5)), 1.0, 0.0).astype(BF)
        down = lax.broadcasted_iota(jnp.int32, (w, 128), 0).astype(F32).astype(BF)
        along = lax.broadcasted_iota(jnp.int32, (16, w), 1).astype(F32).astype(BF)
        scores[t : t + w, 0:128] = dot(hit, down) + float(t)
        line[:, t : t + w] = (
            lax.dot_general(along, hit, (((1,), (1,)), ((), ())), preferred_element_type=F32)
            + float(t)
        )[0:8]
    row = lax.broadcasted_iota(jnp.int32, (KM, 128), 0)
    kidx_ref[0:KM, :] = jnp.where(
        row < MAIN * (spot + 1), scores[0:KM, 0:128], scores[MAIN:PATCHES, 0:128]
    )
    base = MAIN * (spot + 1)
    row = lax.broadcasted_iota(jnp.int32, (MAIN, 128), 0)
    place = scores[pl.ds(pl.multiple_of(base, MAIN), MAIN), 0:128] - (
        base + 32 * (row >> 5)
    ).astype(F32)
    row = lax.broadcasted_iota(jnp.int32, (MAIN, MAIN), 0)
    col = lax.broadcasted_iota(jnp.int32, (MAIN, MAIN), 1)
    mix = jnp.where(col == (row & 1) * 32 + (row >> 1), 1.0, 0.0).astype(BF)
    place = dot(mix, place.astype(BF))
    row = lax.broadcasted_iota(jnp.int32, (MAIN, 128), 0)
    kidx_ref[KM:PATCHES, :] = place + (base + 32 * (row & 1)).astype(F32)
    window = line[0:1, pl.ds(pl.multiple_of(z * QM, QM), QM + 128)]
    col = lax.broadcasted_iota(jnp.int32, (1, QM), 1) + z * QM
    qidx_ref[...] = jnp.where(col < base, window[:, 0:QM], window[:, MAIN : MAIN + QM])
    row = lax.broadcasted_iota(jnp.int32, (MAIN, QO), 0)
    col = lax.broadcasted_iota(jnp.int32, (MAIN, QO), 1)
    mine = jnp.where(row == 8 * z + (col & 7), 1.0, 0.0).astype(BF)
    col = lax.broadcasted_iota(jnp.int32, (1, QO), 1)
    qoidx_ref[...] = dot_t(place.astype(BF), mine)[0:1] + (base + 32 * (col & 1)).astype(F32)

    for i, ref in enumerate((k_ref, v_ref)):
        for k in range(NZ):
            ref[k * QM : (k + 1) * QM, :] = kv_ref[i, k, :, 0:MAIN, :].reshape(QM, HEAD)
            for j in range(NY):
                at = KM + 2 * (k * NY + j)
                ref[at : at + 2, :] = kv_ref[i, k, j, MAIN : MAIN + 2, :]
    kt[...] = k_ref[...].astype(F32).T.astype(BF)
    vt[...] = v_ref[...].astype(F32).T.astype(BF)
    dk[...] = jnp.zeros_like(dk)
    dv[...] = jnp.zeros_like(dv)

    row = lax.broadcasted_iota(jnp.int32, (QM, 512), 0)
    col = lax.broadcasted_iota(jnp.int32, (QM, 512), 1)
    late = jnp.where(z * NY + (row >> 6) > spot, 2, 0)
    pick = jnp.where(col == (row & 31) * 16 + (row >> 5) + late, 1.0, 0.0).astype(BF)
    g_ref[...] = dot(pick, gz_ref[...].reshape(512, 512)).astype(BF)
    row = lax.broadcasted_iota(jnp.int32, (16, 66), 0)
    col = lax.broadcasted_iota(jnp.int32, (16, 66), 1)
    pick = jnp.where((col == 2 * spot + 2 + row) & (row < 2), 1.0, 0.0).astype(BF)
    for j in range(NY):
        extra = dot(pick, gy_ref[j]).astype(BF)
        for h in range(4):
            at = 8 * h + 2 * j
            go_ref[at : at + 2, :] = extra[0:2, HEAD * h : HEAD * (h + 1)]
            qo_ref[at : at + 2, :] = heads_ref[h, j, MAIN : MAIN + 2, :]

    def span(c):
        return pl.ds(pl.multiple_of(c * CHUNK, 32), CHUNK)

    def block(q, g, qidx, width):
        qt = q.astype(F32).T.astype(BF)
        gt32 = g.astype(F32).T
        gt = gt32.astype(BF)

        peak = jnp.full((1, width), -jnp.inf, F32)
        for c in range(chunks):
            at = span(c)
            s = dot(k_ref[at, :], qt) * FACTOR
            index = kidx_ref[at, :]
            index = jnp.concatenate([index, index], axis=1) if width > 128 else index[:, :width]
            s = jnp.where(index <= qidx, s, -jnp.inf)
            scores[at, :width] = s
            peak = jnp.maximum(peak, jnp.max(s, axis=0, keepdims=True))
        total = jnp.zeros((1, width), F32)
        for c in range(chunks):
            at = span(c)
            p = jnp.exp(scores[at, :width] - peak)
            scores[at, :width] = p
            total = total + jnp.sum(p, axis=0, keepdims=True)
        inverse = 1.0 / total
        out_t = jnp.zeros((HEAD, width), F32)
        for c in range(chunks):
            at = span(c)
            a = scores[at, :width] * inverse
            scores[at, :width] = a
            low = a.astype(BF)
            out_t = out_t + dot(vt[:, c * CHUNK : (c + 1) * CHUNK], low)
            dv[at, :] += dot(low, g)
        delta = jnp.sum(gt32 * out_t, axis=0, keepdims=True)
        dq_t = jnp.zeros((HEAD, width), F32)
        for c in range(chunks):
            at = span(c)
            da = dot(v_ref[at, :], gt)
            ds = (scores[at, :width] * (da - delta)).astype(BF)
            dq_t = dq_t + dot(kt[:, c * CHUNK : (c + 1) * CHUNK], ds)
            dk[at, :] += dot(ds, q)
        return out_t, (dq_t * FACTOR).T.astype(BF)

    row = lax.broadcasted_iota(jnp.int32, (QM, QM), 0)
    col = lax.broadcasted_iota(jnp.int32, (QM, QM), 1)
    turn = jnp.where(col == (row & 7) * 32 + (row >> 3), 1.0, 0.0).astype(BF)

    @pl.loop(0, 4)
    def _(h):
        q = heads_ref[h, :, 0:MAIN, :].reshape(QM, HEAD)
        out_t, dq = block(q, g_ref[:, lanes(h)], qidx_ref[...], QM)
        moved = lax.dot_general(
            turn, out_t.astype(BF), (((1,), (1,)), ((), ())), preferred_element_type=F32
        )
        om_ref[:, :, lanes(h)] = moved.astype(BF).reshape(NS, 8, HEAD)
        dq_ref[h, :, 0:MAIN, :] = dq.reshape(NY, MAIN, HEAD)

    out_t, dq = block(qo_ref[...], go_ref[...], qoidx_ref[...], QO)
    out = out_t.T.astype(BF)
    oo_ref[...] = jnp.zeros_like(oo_ref)
    dq_ref[:, :, MAIN:ROWS, :] = jnp.zeros((4, NY, ROWS - MAIN, HEAD), BF)
    for h in range(4):
        for j in range(NY):
            at = 8 * h + 2 * j
            oo_ref[j, 0:2, HEAD * h : HEAD * (h + 1)] = out[at : at + 2]
            dq_ref[h, j, MAIN : MAIN + 2, :] = dq[at : at + 2]
    for i, (ref, scale) in enumerate(((dk, FACTOR), (dv, 1.0))):
        for k in range(NZ):
            block_rows = (ref[k * QM : (k + 1) * QM, :] * scale).astype(BF)
            dkv_ref[i, k, :, 0:MAIN, :] = block_rows.reshape(NY, MAIN, HEAD)
        extra = (ref[KM:PATCHES, :] * scale).astype(BF)
        dkv_ref[i, :, :, MAIN:ROWS, :] = jnp.zeros((NZ, NY, ROWS - MAIN, HEAD), BF)
        for k in range(NZ):
            for j in range(NY):
                at = 2 * (k * NY + j)
                dkv_ref[i, k, j, MAIN : MAIN + 2, :] = extra[at : at + 2]


def attention(heads, kv, gy, gz, spot, owner):
    return pl.pallas_call(
        attention_kernel,
        in_specs=[VM] * 4 + [pl.BlockSpec(memory_space=pltpu.SMEM), VM],
        out_specs=[VM] * 4,
        out_shape=[
            jax.ShapeDtypeStruct((NS, 8, 512), BF),
            jax.ShapeDtypeStruct((NY, 8, 512), BF),
            jax.ShapeDtypeStruct((4, NY, ROWS, HEAD), BF),
            jax.ShapeDtypeStruct((2, NZ, NY, ROWS, HEAD), BF),
        ],
        scratch_shapes=[
            pltpu.VMEM((PATCHES, HEAD), BF),
            pltpu.VMEM((PATCHES, HEAD), BF),
            pltpu.VMEM((HEAD, PATCHES), BF),
            pltpu.VMEM((HEAD, PATCHES), BF),
            pltpu.VMEM((QM, 512), BF),
            pltpu.VMEM((QO, HEAD), BF),
            pltpu.VMEM((QO, HEAD), BF),
            pltpu.VMEM((PATCHES, QM), F32),
            pltpu.VMEM((PATCHES, HEAD), F32),
            pltpu.VMEM((PATCHES, HEAD), F32),
            pltpu.VMEM((PATCHES, 128), F32),
            pltpu.VMEM((8, 2304), F32),
            pltpu.VMEM((1, QM), F32),
            pltpu.VMEM((1, QO), F32),
        ],
        compiler_params=pltpu.CompilerParams(vmem_limit_bytes=VMEM_LIMIT),
        name="attention",
    )(heads, kv, gy, gz, spot, owner)


def columns_kernel(
    dq, dkv, cols, ubuf, usum, dbuf, dsum, red, hs, hr, rs, rr, ls, lr
):
    z, y, x, c = here()
    n = x * 2 + c
    up, down = lax.rem(z + 1, NZ), lax.rem(z + NZ - 1, NZ)
    peers = []
    for j in range(1, NDP * NY):
        p, q = lax.rem(n + j // NY, NDP), lax.rem(y + j, NY)
        peers.append({"y": q, "x": p // 2, "c": lax.rem(p, 2)})
    greet(peers + [{"z": up}, {"z": down}])

    def plan(slot, j):
        k = lax.rem(y + j, NY)
        head = y * 4 + slot if slot < 4 else slot * 4 + y
        d, i = head // 3, lax.rem(head, 3)
        src = dq.at[slot, k] if slot < 4 else red.at[slot - 4, k]
        dst = cols.at[n, :, lanes(i)]
        there = lambda: send(
            src, dst, (hs.at[slot, j], hr.at[n, i]), y=k, x=d // 2, c=lax.rem(d, 2)
        )
        stay = lambda: pltpu.make_async_copy(src, dst, hr.at[n, i])
        return there, stay, d == n

    def start(slot):
        for j in range(1, NY):
            plan(slot, j)[0]().start()
        there, stay, own = plan(slot, 0)

        @pl.when(own)
        def _():
            stay().start()

        @pl.when(jnp.logical_not(own))
        def _():
            there().start()

    def sent(slot):
        for j in range(1, NY):
            plan(slot, j)[0]().wait_send()
        there, _, own = plan(slot, 0)

        @pl.when(jnp.logical_not(own))
        def _():
            there().wait_send()

    def at(k):
        return lax.rem(z + k, NZ)

    ups, downs = {}, {}
    for t in range(1, 5):
        for i in range(2):
            if t == 1:
                above, below = dkv.at[i, at(4)], dkv.at[i, at(5)]
            else:
                ups[t - 1, i].wait_recv()
                usum[i, t - 2] = add(ubuf[i, t - 2], dkv[i, at(5 - t)])
                above = usum.at[i, t - 2]
                if t < 4:
                    downs[t - 1, i].wait_recv()
                    dsum[i, t - 2] = add(dbuf[i, t - 2], dkv[i, at(4 + t)])
                    below = dsum.at[i, t - 2]
            ups[t, i] = send(above, ubuf.at[i, t - 1], (rs.at[t - 1, i], rr.at[t - 1, i]), z=up)
            ups[t, i].start()
            if t < 4:
                downs[t, i] = send(
                    below, dbuf.at[i, t - 1], (ls.at[t - 1, i], lr.at[t - 1, i]), z=down
                )
                downs[t, i].start()
        if t == 1:
            for slot in range(4):
                start(slot)
    for i in range(2):
        downs[3, i].wait_recv()
        ups[4, i].wait_recv()
        red[i] = add(ubuf[i, 3], dbuf[i, 2], dkv[i, z])
        start(4 + i)
    for p in range(NDP):
        for i in range(3):
            block = cols.at[p, :, i * HEAD : (i + 1) * HEAD]
            pltpu.make_async_copy(block, block, hr.at[p, i]).wait()
    for copy in (*ups.values(), *downs.values()):
        copy.wait_send()
    for slot in range(6):
        sent(slot)


def to_columns(dq, dkv):
    dma = pltpu.SemaphoreType.DMA
    part = (NY, ROWS, HEAD)
    return pl.pallas_call(
        columns_kernel,
        in_specs=[VM, VM],
        out_specs=ANY,
        out_shape=jax.ShapeDtypeStruct((NDP, ROWS, COLS), BF),
        scratch_shapes=[
            pltpu.VMEM((2, 4, *part), BF),
            pltpu.VMEM((2, 3, *part), BF),
            pltpu.VMEM((2, 3, *part), BF),
            pltpu.VMEM((2, 2, *part), BF),
            pltpu.VMEM((2, *part), BF),
            dma((6, NY)),
            dma((NDP, 3)),
            dma((4, 2)),
            dma((4, 2)),
            dma((3, 2)),
            dma((3, 2)),
        ],
        compiler_params=pltpu.CompilerParams(
            collective_id=2, has_side_effects=True, vmem_limit_bytes=VMEM_LIMIT
        ),
        name="to_columns",
    )(dq, dkv)


def products_kernel(
    main_ref, over_ref, cols_ref, weight_ref,
    part_ref, back_ref, extra_ref,
    cm, co, cmt, cot, over_rows,
):
    @pl.when(pl.program_id(0) == 0)
    def _():
        for n in range(NDP):
            cm[MAIN * n : MAIN * (n + 1), :] = cols_ref[n, 0:MAIN, :]
            co[2 * n : 2 * n + 2, :] = cols_ref[n, MAIN : MAIN + 2, :]
        cmt[...] = cm[...].astype(F32).T.astype(BF)
        cot[...] = co[...].astype(F32).T.astype(BF)

    width = weight_ref.shape[0]
    for n in range(NDP):
        over_rows[2 * n : 2 * n + 2, :] = over_ref[n]
    part = dot(cmt[...], main_ref[...].reshape(NDP * MAIN, width)) + dot(cot[...], over_rows[...])
    part = part.astype(BF)
    for k in range(NY):
        part_ref[0, k] = part[:, HEAD * k : HEAD * (k + 1)]
    turn = (((1,), (1,)), ((), ()))
    back = lax.dot_general(cm[...], weight_ref[...], turn, preferred_element_type=F32)
    back_ref[...] = back.astype(BF).reshape(NDP, MAIN, width)
    extra = lax.dot_general(co[...], weight_ref[...], turn, preferred_element_type=F32)
    extra = extra.astype(BF)
    for n in range(NDP):
        extra_ref[n] = extra[2 * n : 2 * n + 2]


def products(all_main, all_over, cols, weight):
    steps = NZ
    width = DG // steps
    return pl.pallas_call(
        products_kernel,
        grid=(steps,),
        in_specs=[
            pl.BlockSpec((NDP, MAIN, width), lambda i: (0, 0, i)),
            pl.BlockSpec((NDP, 2, width), lambda i: (0, 0, i)),
            pl.BlockSpec((NDP, ROWS, COLS), lambda i: (0, 0, 0)),
            pl.BlockSpec((width, COLS), lambda i: (i, 0)),
        ],
        out_specs=[
            pl.BlockSpec((1, NY, COLS, HEAD), lambda i: (i, 0, 0, 0)),
            pl.BlockSpec((NDP, MAIN, width), lambda i: (0, 0, i)),
            pl.BlockSpec((NDP, 2, width), lambda i: (0, 0, i)),
        ],
        out_shape=[
            jax.ShapeDtypeStruct((NZ, NY, COLS, HEAD), BF),
            jax.ShapeDtypeStruct((NDP, MAIN, DG), BF),
            jax.ShapeDtypeStruct((NDP, 2, DG), BF),
        ],
        scratch_shapes=[
            pltpu.VMEM((NDP * MAIN, COLS), BF),
            pltpu.VMEM((16, COLS), BF),
            pltpu.VMEM((COLS, NDP * MAIN), BF),
            pltpu.VMEM((COLS, 16), BF),
            pltpu.VMEM((16, width), BF),
        ],
        compiler_params=pltpu.CompilerParams(vmem_limit_bytes=VMEM_LIMIT),
        name="products",
    )(all_main, all_over, cols, weight)


LONG = 256
SHORT = COLS - LONG


def sums_kernel(
    back, extra, w, om, oo,
    pooled, over_all, wgrad, am, ao,
    own, sib, chip, xa, xb, xr, xl, sxa, sxb,
    ya, yb, yr, yl, sa, sb, wy, wz, ubuf, usum, dbuf, dsum, wb, wq, obuf, omz, ov, oz,
    local, cs, cr, xs, xrv, ws, wr, us, ur, ds, dr, zs, zr, os_, or_, ps, pr,
):
    z, y, x, c = here()
    n = x * 2 + c
    right, left, far = lax.rem(x + 1, NX), lax.rem(x + 3, NX), lax.rem(x + 2, NX)
    yn, yp, yf = lax.rem(y + 1, NY), lax.rem(y + 3, NY), lax.rem(y + 2, NY)
    up, down = lax.rem(z + 1, NZ), lax.rem(z + NZ - 1, NZ)
    ys_at = [lax.rem(y + j, NY) for j in range(NY)]
    zs_at = [lax.rem(z + j, NZ) for j in range(NZ)]
    dp_at = [lax.rem(n + j, NDP) for j in range(NDP)]
    greet(
        [{"y": ys_at[j]} for j in range(1, NY)]
        + [{"z": zs_at[j]} for j in range(1, NZ)]
        + [{"x": p // 2, "c": lax.rem(p, 2)} for p in dp_at[1:]]
    )
    copies, stays = [], []

    def go(src, dst, pair, **device):
        copy = send(src, dst, pair, **device)
        copy.start()
        copies.append(copy)
        return copy

    def stay(src, dst):
        copy = pltpu.make_async_copy(src, dst, local.at[len(stays)])
        copy.start()
        stays.append(copy)
        return copy

    waited = []

    def done(copy):
        copy.wait()
        waited.append(copy)

    def at(k):
        return lax.rem(z + k, NZ)

    order = (far, right, left, x)
    halves = [
        go(back.at[p * 2 + 1 - c], sib.at[p], (cs.at[k], cr.at[k]), c=1 - c)
        for k, p in enumerate(order)
    ]
    loads = [stay(back.at[p * 2 + c], own.at[p]) for p in order]

    overs = [
        go(extra.at[p], obuf.at[n], (ps.at[j], pr.at[j]), x=p // 2, c=lax.rem(p, 2))
        for j, p in enumerate(dp_at)
        if j
    ]
    here_o = stay(extra.at[n], obuf.at[n])

    short, long = pl.ds(LONG, SHORT), pl.ds(0, LONG)
    ups, downs = {}, {}

    def ring(t):
        for i in range(2):
            some = pl.ds(2 * i, 2)
            if t == 1:
                above, below = w.at[at(4), some, short], w.at[at(5), some, short]
            else:
                ups[t - 1, i].wait_recv()
                usum[t - 2, i] = add(ubuf[t - 2, i], w[at(5 - t), some, short])
                above = usum.at[t - 2, i]
                if t < 4:
                    downs[t - 1, i].wait_recv()
                    dsum[t - 2, i] = add(dbuf[t - 2, i], w[at(4 + t), some, short])
                    below = dsum.at[t - 2, i]
            ups[t, i] = go(above, ubuf.at[t - 1, i], (us.at[t - 1, i], ur.at[t - 1, i]), z=up)
            if t < 4:
                downs[t, i] = go(
                    below, dbuf.at[t - 1, i], (ds.at[t - 1, i], dr.at[t - 1, i]), z=down
                )

    ring(1)
    lo, hi = pl.ds(0, 4), pl.ds(4, 4)
    w_a = go(w.at[lo, yf, long], ya, (ws.at[0], wr.at[0]), y=yn)
    w_b = go(w.at[hi, yf, long], yb, (ws.at[1], wr.at[1]), y=yp)
    w_hi = go(w.at[hi, yn, long], yr.at[hi], (ws.at[2], wr.at[2]), y=yn)
    w_lo = go(w.at[lo, yp, long], yl.at[lo], (ws.at[3], wr.at[3]), y=yp)

    first, second = pl.ds(0, DG // 2), pl.ds(DG // 2, DG // 2)
    for k, p in enumerate(order):
        done(loads[k])
        halves[k].wait_recv()
        chip[p] = add(own[p], sib[p])
        if k == 0:
            x_a = go(chip.at[p, :, first], xa, (xs.at[0], xrv.at[0]), x=right)
            x_b = go(chip.at[p, :, second], xb, (xs.at[1], xrv.at[1]), x=left)
        if k == 1:
            x_hi = go(chip.at[p, :, second], xr.at[:, second], (xs.at[2], xrv.at[2]), x=right)
        if k == 2:
            x_lo = go(chip.at[p, :, first], xl.at[:, first], (xs.at[3], xrv.at[3]), x=left)

    for copy in overs:
        copy.wait_recv()
    done(here_o)
    ov[...] = add(*[obuf[k] for k in range(NDP)])
    over_z = [go(ov, oz.at[z], (zs.at[1, j], zr.at[1, j]), z=zs_at[j]) for j in range(1, NZ)]
    keep_oz = stay(ov, oz.at[z])
    ring(2)
    w_a.wait_recv()
    sa[...] = add(ya[...], w[lo, yn, long])
    w_lo2 = go(sa, yr.at[lo], (ws.at[4], wr.at[4]), y=yn)
    w_b.wait_recv()
    sb[...] = add(yb[...], w[hi, yp, long])
    w_hi2 = go(sb, yl.at[hi], (ws.at[5], wr.at[5]), y=yp)
    ring(3)
    x_a.wait_recv()
    sxa[...] = add(xa[...], chip[right, :, first])
    x_lo2 = go(sxa, xr.at[:, first], (xs.at[4], xrv.at[4]), x=right)
    x_b.wait_recv()
    sxb[...] = add(xb[...], chip[left, :, second])
    x_hi2 = go(sxb, xl.at[:, second], (xs.at[5], xrv.at[5]), x=left)
    for copy in over_z:
        copy.wait_recv()
    done(keep_oz)
    over_y = [
        go(oz, over_all.at[y], (os_.at[2, j], or_.at[2, j]), y=ys_at[j]) for j in range(1, NY)
    ]
    stay(oz, over_all.at[y])
    ring(4)
    rows_z = [
        go(om.at[zs_at[j]], omz.at[z], (zs.at[0, j], zr.at[0, j]), z=zs_at[j])
        for j in range(1, NZ)
    ]
    here_z = stay(om.at[z], omz.at[z])

    for copy in (w_hi, w_lo, w_lo2, w_hi2):
        copy.wait_recv()
    wy[...] = add(w[:, y, long], yr[...], yl[...])
    longs = [
        go(wy.at[zs_at[j]], wz.at[j], (zs.at[2, j], zr.at[2, j]), z=zs_at[j])
        for j in range(1, NZ)
    ]
    for i in range(2):
        downs[3, i].wait_recv()
        ups[4, i].wait_recv()
        some = pl.ds(2 * i, 2)
        wb[some] = add(w[z, some, short], ubuf[3, i], dbuf[2, i])
    shorts = [
        go(wb.at[ys_at[j]], wq.at[j], (os_.at[3, j], or_.at[3, j]), y=ys_at[j])
        for j in range(1, NY)
    ]

    for copy in rows_z:
        copy.wait_recv()
    done(here_z)
    rows_y = []
    for j in range(1, NY):
        k = ys_at[j]
        rows_y.append(go(omz.at[:, k], am.at[y], (os_.at[0, j], or_.at[0, j]), y=k))
        rows_y.append(go(oo.at[k], ao.at[y], (os_.at[1, j], or_.at[1, j]), y=k))
    stay(omz.at[:, y], am.at[y])
    stay(oo.at[y], ao.at[y])

    for copy in (x_hi, x_lo, x_lo2, x_hi2):
        copy.wait_recv()
    pooled[...] = add(chip[x], xr[...], xl[...])
    for copy in shorts:
        copy.wait_recv()
    total = wb[y].astype(F32)
    for j in range(1, NY):
        total = total + wq[j].astype(F32)
    wgrad[short, :] = total
    for copy in longs:
        copy.wait_recv()
    total = wy[z].astype(F32)
    for j in range(1, NZ):
        total = total + wz[j].astype(F32)
    wgrad[long, :] = total
    for copy in (*over_y, *rows_y):
        copy.wait_recv()
    for copy in copies:
        copy.wait_send()
    for copy in stays:
        if not any(copy is other for other in waited):
            copy.wait()


def sums(back, extra, part, om, oo):
    dma = pltpu.SemaphoreType.DMA
    rows = (MAIN, DG)
    half = (MAIN, DG // 2)
    long = (LONG, HEAD)
    short = (2, SHORT, HEAD)
    return pl.pallas_call(
        sums_kernel,
        in_specs=[ANY, ANY, VM, VM, VM],
        out_specs=[VM, ANY, VM, ANY, VM],
        out_shape=[
            jax.ShapeDtypeStruct(rows, BF),
            jax.ShapeDtypeStruct((NY, NZ, 2, DG), BF),
            jax.ShapeDtypeStruct((COLS, HEAD), F32),
            jax.ShapeDtypeStruct((NY, NZ, 8, 512), BF),
            jax.ShapeDtypeStruct((NY, 8, 512), BF),
        ],
        scratch_shapes=[
            *[pltpu.VMEM((NX, *rows), BF)] * 3,
            *[pltpu.VMEM(half, BF)] * 2,
            *[pltpu.VMEM(rows, BF)] * 2,
            *[pltpu.VMEM(half, BF)] * 2,
            *[pltpu.VMEM((4, *long), BF)] * 2,
            *[pltpu.VMEM((8, *long), BF)] * 2,
            *[pltpu.VMEM((4, *long), BF)] * 2,
            *[pltpu.VMEM((8, *long), BF)] * 2,
            pltpu.VMEM((4, 2, *short), BF),
            pltpu.VMEM((3, 2, *short), BF),
            pltpu.VMEM((3, 2, *short), BF),
            pltpu.VMEM((2, 2, *short), BF),
            pltpu.VMEM((4, SHORT, HEAD), BF),
            pltpu.VMEM((4, SHORT, HEAD), BF),
            pltpu.VMEM((NDP, 2, DG), BF),
            pltpu.VMEM((NZ, NY, 8, 512), BF),
            pltpu.VMEM((2, DG), BF),
            pltpu.VMEM((NZ, 2, DG), BF),
            dma((10,)),
            dma((4,)),
            dma((4,)),
            dma((6,)),
            dma((6,)),
            dma((6,)),
            dma((6,)),
            dma((4, 2)),
            dma((4, 2)),
            dma((3, 2)),
            dma((3, 2)),
            dma((3, NZ)),
            dma((3, NZ)),
            dma((4, NY)),
            dma((4, NY)),
            dma((NDP,)),
            dma((NDP,)),
        ],
        compiler_params=pltpu.CompilerParams(
            collective_id=3, has_side_effects=True, vmem_limit_bytes=VMEM_LIMIT
        ),
        name="sums",
    )(back, extra, part, om, oo)


def body(byte_states, byte_patch, patch_owner, qkv_weight, attention_output_gradient):
    main, over, slot, flag, band = pool(
        byte_patch, patch_owner, byte_states, attention_output_gradient
    )
    all_main, all_over, spot, gy, gz, heads, kv = front(
        main, over, flag, band, attention_output_gradient, qkv_weight
    )
    om, oo, dq, dkv = attention(heads, kv, gy, gz, spot, patch_owner)
    cols = to_columns(dq, dkv)
    part, back, extra = products(all_main, all_over, cols, qkv_weight)
    om = om.reshape(NZ, NY, 8, 512)
    pooled, over_back, wide, am, ao = sums(back, extra, part, om, oo)
    state_grad, att, weight_grad = spread(slot, pooled, over_back, am, ao, spot, wide)
    return att, state_grad, weight_grad


def solution(mesh):
    finer = Mesh(mesh.devices.reshape(NZ, NY, NX, NC), ("z", "y", "x", "c"))
    placed = (P(DP, SEQ, None), P(DP, SEQ), P(DP, None), P(None, DP), P(DP, SEQ, None))
    return jax.shard_map(
        body,
        mesh=finer,
        in_specs=placed,
        out_specs=(P(DP, SEQ, None), P(DP, SEQ, None), P(SEQ, DP)),
        check_vma=False,
    )
```
